32 devices in a mesh: band: 8 (over z, y), mem: 4 (over x, core).
Axes of the slice: x: 2, y: 2, z: 4, core: 2. Of those that a mesh axis runs over, the one named last changes fastest.
Arguments:
- ensemble: float32 [128, 5, 32, 128], P('mem', None, 'band'), may hold values from -5 to 5
- obs_value: float32 [256, 128], P(('band', 'mem')), may hold values from -6 to 6
- obs_site: int32 [256, 128], P(('band', 'mem')), may hold values from 0 to 79
- obs_count: int32 [256], P(('band', 'mem')), may hold values from 32 to 128
- obs_precision: float32 [256, 128], P(('band', 'mem')), may hold values from 0.25 to 4
- loc_weight: float32 [256, 3], P(('band', 'mem')), may hold values from 0.1 to 1
- neighbours: int32 [256, 3], P(('band', 'mem')), may hold values from 0 to 7
Outputs:
- forecast: float32 [128, 5, 32, 128], P('mem', None, 'band')
The draws below stay inside these ranges and needn't reach their ends.
Inputs may be any that keep to these rules, and one draw needn't show every extreme that they name: `obs_site`: site v * 16 + c observes variable v at the tile's c-th cell. Slots 0 to obs_count - 1 of a tile are live. `neighbours`: entries are positions within the aligned block of 8 tiles that holds the tile.
All inputs are finite; a program needn't handle non-finite values.
Results may differ from the reference program's by a relative error of at most 0.0003.
Values sent between devices are 32-bit elements; how exact they have to be, the bound alone decides.
A program may use at most 64 MiB of HBM per device.

```python
import math
import jax
import jax.numpy as jnp
from jax import lax

M = 128
V = 5
NLON = 128
TILE = 16
OBS = 128
NB = 3
NSI = 6
STEPS = 2
NLAT = 32
TILES = 256
TILES_A = 8


def set_ends(result, rng, least, high):
    spot = [jax.random.randint(jax.random.fold_in(rng, axis), (), 0, length) for axis, length in enumerate(result.shape)]
    main_axis = result.shape.index(max(result.shape))
    beside = spot[:main_axis] + [(spot[main_axis] + 1) % result.shape[main_axis]] + spot[main_axis + 1:]
    return result.at[tuple(spot)].set(least).at[tuple(beside)].set(high)


def block_scale(key, shape, shards, smallest, top_value):
    def one(position, blocks):
        draws = jax.random.uniform(jax.random.fold_in(jax.random.fold_in(key, 6), position), (blocks,), jnp.float32, smallest / len(shards), top_value / len(shards))
        return jnp.repeat(jnp.exp(draws), shape[position] // blocks).reshape((-1,) + (1,) * (len(shape) - position - 1))

    loudness = one(*shards[0])
    for cut in shards[1:]:
        loudness = loudness * one(*cut)
    return loudness


def normal_values(own_key, shape, width, limit, shards=(), held_as=jnp.bfloat16):
    level = block_scale(own_key, shape, shards, -0.22, 0.18) if shards else 1.0
    entries = jax.random.normal(own_key, shape, jnp.float32) * width * level
    return jnp.minimum(jnp.maximum(entries, -limit), limit).astype(held_as)


def setup_inputs(seed: int = 0) -> dict:
    streams_of = jax.random.split(jax.random.key(seed), 8)
    return {
        "ensemble": normal_values(streams_of[0], (M, V, NLAT, NLON), 1.0, 5.0, ((0, 4), (2, 8)), jnp.float32),
        "obs_value": normal_values(streams_of[1], (TILES, OBS), 1.5, 6.0, ((0, 32),), jnp.float32),
        "obs_site": set_ends(jax.random.randint(streams_of[2], (TILES, OBS), 0, V * TILE), jax.random.fold_in(streams_of[2], 1), 0, (V * TILE) - 1).astype(jnp.int32),
        "obs_count": set_ends(jax.random.randint(streams_of[3], (TILES,), OBS // 4, OBS + 1), jax.random.fold_in(streams_of[3], 1), OBS // 4, OBS).astype(jnp.int32),
        "obs_precision": jnp.clip(jnp.exp(math.log(4.0) - 2.7725887 * jax.random.uniform(streams_of[4], (TILES, OBS), jnp.float32) ** block_scale(streams_of[4], (TILES, OBS), ((0, 32),), -0.2, 0.2)), 0.25, 4.0),
        "loc_weight": jnp.clip(jnp.exp(math.log(1.0) - 2.3025851 * jax.random.uniform(streams_of[5], (TILES, NB), jnp.float32) ** block_scale(streams_of[5], (TILES, NB), ((0, 32),), -0.2, 0.2)), 0.1, 1.0),
        "neighbours": set_ends(jax.random.randint(streams_of[6], (TILES, NB), 0, TILES_A), jax.random.fold_in(streams_of[6], 1), 0, TILES_A - 1).astype(jnp.int32),
    }


COURANT = 0.08
HIGHEST = lax.Precision.HIGHEST

def minmod(lower_jump, upper_jump):
    return jnp.maximum(0.0, jnp.minimum(lower_jump, upper_jump)) + jnp.minimum(0.0, jnp.maximum(lower_jump, upper_jump))

def flux_divergence(halo_extended_field, sweep_direction, advected_field):
    extent = halo_extended_field.shape[sweep_direction]
    differences = lax.slice_in_dim(halo_extended_field, 1, extent, axis=sweep_direction) - lax.slice_in_dim(halo_extended_field, 0, extent - 1, axis=sweep_direction)
    slopes = minmod(lax.slice_in_dim(differences, 0, extent - 2, axis=sweep_direction), lax.slice_in_dim(differences, 1, extent - 1, axis=sweep_direction))
    state_left_side = lax.slice_in_dim(halo_extended_field, 1, extent - 2, axis=sweep_direction) + 0.5 * lax.slice_in_dim(slopes, 0, extent - 3, axis=sweep_direction)
    state_right_side = lax.slice_in_dim(halo_extended_field, 2, extent - 1, axis=sweep_direction) - 0.5 * lax.slice_in_dim(slopes, 1, extent - 2, axis=sweep_direction)
    advected_field_left = state_left_side[:, advected_field:advected_field + 1]
    advected_field_right = state_right_side[:, advected_field:advected_field + 1]
    signal_velocity = jnp.maximum(jnp.abs(advected_field_left), jnp.abs(advected_field_right))
    interface_fluxes = 0.5 * (advected_field_left * state_left_side + advected_field_right * state_right_side) - 0.5 * signal_velocity * (state_right_side - state_left_side)
    return lax.slice_in_dim(interface_fluxes, 1, extent - 3, axis=sweep_direction) - lax.slice_in_dim(interface_fluxes, 0, extent - 4, axis=sweep_direction)

def advance(halo_extended_field):
    centre = halo_extended_field[:, :, 2:-2]
    lat_div = flux_divergence(halo_extended_field, 2, 1)
    wrapped = jnp.concatenate([centre[..., -2:], centre, centre[..., :2]], axis=3)
    lon_div = flux_divergence(wrapped, 3, 0)
    return centre - COURANT * (lat_div + lon_div)

def obs_space(tile_state, obs_value, obs_site):
    site_count = tile_state.shape[2]
    ens_mean = lax.optimization_barrier(jnp.mean(tile_state, axis=1))
    anomaly = tile_state - ens_mean[:, None, :]
    selector = (obs_site[:, :, None] == jnp.arange(site_count)[None, None, :]).astype(jnp.float32)
    obs_anomaly = jnp.einsum('bos,bks->bok', selector, anomaly, precision=HIGHEST)
    obs_mean = jnp.einsum('bos,bs->bo', selector, ens_mean, precision=HIGHEST)
    return (ens_mean, anomaly, obs_anomaly, obs_value - obs_mean)

def transform(local_anomaly, local_innovation, local_weight, ens_mean, anomaly):
    members = local_anomaly.shape[2]
    identity = jnp.eye(members, dtype=jnp.float32)
    weighted = local_anomaly * local_weight[:, :, None]
    gram_matrix = jnp.einsum('bpk,bpj->bkj', weighted, local_anomaly, precision=HIGHEST) + (members - 1.0) * identity
    frob_norm = jnp.sqrt(lax.optimization_barrier(jnp.sum(gram_matrix * gram_matrix, axis=(1, 2))))
    root_iter = gram_matrix / frob_norm[:, None, None]
    inverse = jnp.broadcast_to(identity, gram_matrix.shape)
    for sweep in range(NSI):
        factor = 1.5 * identity - 0.5 * jnp.matmul(inverse, root_iter, precision=HIGHEST)
        root_iter = jnp.matmul(root_iter, factor, precision=HIGHEST)
        inverse = jnp.matmul(factor, inverse, precision=HIGHEST)
    projected = jnp.einsum('bpk,bp->bk', weighted, local_innovation, precision=HIGHEST)
    halfway = jnp.einsum('bkj,bj->bk', inverse, projected, precision=HIGHEST)
    mean_weights = jnp.einsum('bkj,bj->bk', inverse, halfway, precision=HIGHEST) / frob_norm[:, None]
    spread_weights = inverse * jnp.sqrt((members - 1.0) / frob_norm)[:, None, None]
    combined = spread_weights + mean_weights[:, :, None]
    return ens_mean[:, None, :] + jnp.einsum('bjk,bjs->bks', combined, anomaly, precision=HIGHEST)

def localise(obs_anomaly, innovation, slot_weight, neighbour_tiles, loc_weight, ens_mean, anomaly):
    batch_tiles = neighbour_tiles.shape[0]
    local_anomaly = obs_anomaly[neighbour_tiles].reshape(batch_tiles, -1, obs_anomaly.shape[2])
    local_innovation = innovation[neighbour_tiles].reshape(batch_tiles, -1)
    local_weight = (loc_weight[:, :, None] * slot_weight[neighbour_tiles]).reshape(batch_tiles, -1)
    return transform(local_anomaly, local_innovation, local_weight, ens_mean, anomaly)

def reference(ensemble, obs_value, obs_site, obs_count, obs_precision, loc_weight, neighbours):
    fields = ensemble
    for repeat in range(STEPS):
        fields = advance(jnp.pad(fields, ((0, 0), (0, 0), (2, 2), (0, 0))))
    members, variables, lat_total, lon_total = fields.shape
    tile_count = lat_total * lon_total // TILE
    tile_state = fields.reshape(members, variables, tile_count, TILE).transpose(2, 0, 1, 3).reshape(tile_count, members, variables * TILE)
    block_size = math.gcd(tile_count, 64)

    def blocked(array):
        return array.reshape((tile_count // block_size, block_size) + array.shape[1:])

    def unblocked(array):
        return array.reshape((tile_count,) + array.shape[2:])

    def space_block(parts):
        return obs_space(parts[0], parts[1], parts[2])
    results = lax.map(space_block, (blocked(tile_state), blocked(obs_value), blocked(obs_site)))
    ens_mean, anomaly, obs_anomaly, innovation = [unblocked(item) for item in results]
    live_slots = jnp.arange(obs_value.shape[1]).astype(jnp.int32)[None, :] < obs_count[:, None]
    slot_weight = jnp.where(live_slots, obs_precision, 0.0)
    neighbour_tiles = (jnp.arange(tile_count) // TILES_A * TILES_A).astype(jnp.int32)[:, None] + neighbours

    def analyse_block(parts):
        return localise(obs_anomaly, innovation, slot_weight, parts[0], parts[1], parts[2], parts[3])
    analysed = unblocked(lax.map(analyse_block, (blocked(neighbour_tiles), blocked(loc_weight), blocked(ens_mean), blocked(anomaly))))
    fields = analysed.reshape(tile_count, members, variables, TILE).transpose(1, 2, 0, 3).reshape(members, variables, lat_total, lon_total)
    return advance(jnp.pad(fields, ((0, 0), (0, 0), (2, 2), (0, 0))))
```

```python
import functools

import jax
import jax.numpy as jnp
from jax import lax
from jax.experimental import pallas as pl
from jax.experimental.pallas import tpu as pltpu
from jax.sharding import PartitionSpec as P

TILE = 16
NSI = 6
STEPS = 2


COURANT = 0.08
HIGHEST = lax.Precision.HIGHEST
MESH = pl.DeviceIdType.MESH


def extended_2(block, sides, width):
    for axis, dim in sides:
        count = lax.axis_size(axis)
        forward = [(i, i + 1) for i in range(count - 1)]
        backward = [(target, source) for source, target in forward]
        low = lax.ppermute(
            lax.slice_in_dim(block, block.shape[dim] - width, None, axis=dim), axis, forward
        )
        high = lax.ppermute(lax.slice_in_dim(block, 0, width, axis=dim), axis, backward)
        block = jnp.concatenate([low, block, high], axis=dim)
    return block


def minmod(lower_jump, upper_jump):
    return jnp.maximum(0.0, jnp.minimum(lower_jump, upper_jump)) + jnp.minimum(
        0.0, jnp.maximum(lower_jump, upper_jump)
    )


def flux_divergence(halo_extended_field, sweep_direction, advected_field):
    extent = halo_extended_field.shape[sweep_direction]
    differences = lax.slice_in_dim(
        halo_extended_field, 1, extent, axis=sweep_direction
    ) - lax.slice_in_dim(halo_extended_field, 0, extent - 1, axis=sweep_direction)
    slopes = minmod(
        lax.slice_in_dim(differences, 0, extent - 2, axis=sweep_direction),
        lax.slice_in_dim(differences, 1, extent - 1, axis=sweep_direction),
    )
    state_left_side = lax.slice_in_dim(
        halo_extended_field, 1, extent - 2, axis=sweep_direction
    ) + 0.5 * lax.slice_in_dim(slopes, 0, extent - 3, axis=sweep_direction)
    state_right_side = lax.slice_in_dim(
        halo_extended_field, 2, extent - 1, axis=sweep_direction
    ) - 0.5 * lax.slice_in_dim(slopes, 1, extent - 2, axis=sweep_direction)
    advected_field_left = state_left_side[:, advected_field : advected_field + 1]
    advected_field_right = state_right_side[:, advected_field : advected_field + 1]
    signal_velocity = jnp.maximum(jnp.abs(advected_field_left), jnp.abs(advected_field_right))
    interface_fluxes = 0.5 * (
        advected_field_left * state_left_side + advected_field_right * state_right_side
    ) - 0.5 * signal_velocity * (state_right_side - state_left_side)
    return lax.slice_in_dim(
        interface_fluxes, 1, extent - 3, axis=sweep_direction
    ) - lax.slice_in_dim(interface_fluxes, 0, extent - 4, axis=sweep_direction)


def advance(halo_extended_field):
    centre = halo_extended_field[:, :, 2:-2]
    lat_div = flux_divergence(halo_extended_field, 2, 1)
    wrapped = jnp.concatenate([centre[..., -2:], centre, centre[..., :2]], axis=3)
    lon_div = flux_divergence(wrapped, 3, 0)
    return centre - COURANT * (lat_div + lon_div)


def obs_space(tile_state, obs_value, obs_site):
    site_count = tile_state.shape[2]
    ens_mean = jnp.mean(tile_state, axis=1)
    anomaly = tile_state - ens_mean[:, None, :]
    selector = (obs_site[:, :, None] == jnp.arange(site_count)[None, None, :]).astype(jnp.float32)
    obs_anomaly = jnp.einsum("bos,bks->bok", selector, anomaly, precision=HIGHEST)
    obs_mean = jnp.einsum("bos,bs->bo", selector, ens_mean, precision=HIGHEST)
    return (ens_mean, anomaly, obs_anomaly, obs_value - obs_mean)


def transform(local_anomaly, local_innovation, local_weight, ens_mean, anomaly):
    members = local_anomaly.shape[2]
    identity = jnp.eye(members, dtype=jnp.float32)
    weighted = local_anomaly * local_weight[:, :, None]
    gram_matrix = (
        jnp.einsum("bpk,bpj->bkj", weighted, local_anomaly, precision=HIGHEST)
        + (members - 1.0) * identity
    )
    frob_norm = jnp.sqrt(jnp.sum(gram_matrix * gram_matrix, axis=(1, 2)))
    root_iter = gram_matrix / frob_norm[:, None, None]
    inverse = jnp.broadcast_to(identity, gram_matrix.shape)
    for sweep in range(NSI):
        factor = 1.5 * identity - 0.5 * jnp.matmul(inverse, root_iter, precision=HIGHEST)
        root_iter = jnp.matmul(root_iter, factor, precision=HIGHEST)
        inverse = jnp.matmul(factor, inverse, precision=HIGHEST)
    projected = jnp.einsum("bpk,bp->bk", weighted, local_innovation, precision=HIGHEST)
    halfway = jnp.einsum("bkj,bj->bk", inverse, projected, precision=HIGHEST)
    mean_weights = (
        jnp.einsum("bkj,bj->bk", inverse, halfway, precision=HIGHEST) / frob_norm[:, None]
    )
    spread_weights = inverse * jnp.sqrt((members - 1.0) / frob_norm)[:, None, None]
    combined = spread_weights + mean_weights[:, :, None]
    return ens_mean[:, None, :] + jnp.einsum("bjk,bjs->bks", combined, anomaly, precision=HIGHEST)


def localise(obs_anomaly, innovation, slot_weight, neighbour_tiles, loc_weight, ens_mean, anomaly):
    batch_tiles = neighbour_tiles.shape[0]
    local_anomaly = obs_anomaly[neighbour_tiles].reshape(batch_tiles, -1, obs_anomaly.shape[2])
    local_innovation = innovation[neighbour_tiles].reshape(batch_tiles, -1)
    local_weight = (loc_weight[:, :, None] * slot_weight[neighbour_tiles]).reshape(batch_tiles, -1)
    return transform(local_anomaly, local_innovation, local_weight, ens_mean, anomaly)


def shards(ensemble, obs_value, obs_site, obs_count, obs_precision, loc_weight, neighbours):
    fields = ensemble
    lat_rows = fields.shape[2]
    margin = 2 * STEPS
    extended = extended_2(fields, (("band", 2),), margin)
    offset = lax.axis_index("band") * lat_rows
    lat_total = lat_rows * lax.axis_size("band")
    for repeat in range(STEPS):
        extended = advance(extended)
        remaining = margin - 2 * (repeat + 1)
        if remaining > 0:
            global_row = (
                lax.broadcasted_iota(jnp.int32, (1, 1, extended.shape[2], 1), 2)
                - remaining
                + offset
            )
            inside = (global_row >= 0) & (global_row < lat_total)
            extended = jnp.where(inside, extended, 0.0)
    fields = extended
    members, variables, lon_total = (fields.shape[0], fields.shape[1], fields.shape[3])
    flattened = fields.reshape(members, variables, lat_rows * lon_total)
    grouped = lax.all_to_all(flattened, "mem", split_axis=2, concat_axis=0, tiled=True)
    all_members = grouped.shape[0]
    tile_count = neighbours.shape[0]
    tile_state = (
        grouped.reshape(all_members, variables, tile_count, TILE)
        .transpose(2, 0, 1, 3)
        .reshape(tile_count, all_members, variables * TILE)
    )
    ens_mean, anomaly, obs_anomaly, innovation = obs_space(tile_state, obs_value, obs_site)
    live_slots = jnp.arange(obs_value.shape[1])[None, :] < obs_count[:, None]
    slot_weight = jnp.where(live_slots, obs_precision, 0.0)
    analysed = localise(
        obs_anomaly, innovation, slot_weight, neighbours, loc_weight, ens_mean, anomaly
    )
    outgoing = (
        analysed.reshape(tile_count, all_members, variables, TILE)
        .transpose(1, 2, 0, 3)
        .reshape(all_members, variables, tile_count * TILE)
    )
    returned = lax.all_to_all(outgoing, "mem", split_axis=0, concat_axis=2, tiled=True)
    fields = returned.reshape(members, variables, lat_rows, lon_total)
    return advance(extended_2(fields, (("band", 2),), 2))


def split_pair(x):
    high = x.astype(jnp.bfloat16)
    low = (x - high.astype(jnp.float32)).astype(jnp.bfloat16)
    return high, low


def left_form(x):
    return jnp.concatenate(split_pair(x), axis=1)


def right_form(x):
    wide = jnp.concatenate(split_pair(x), axis=1)
    return jnp.concatenate([wide, wide], axis=0)


def pair_dot(left, right):
    both = jnp.dot(left, right, preferred_element_type=jnp.float32)
    half = both.shape[1] // 2
    return both[:, :half] + both[:, half:]


def upwind(left, right, carrier):
    a_left = left[carrier : carrier + 1]
    a_right = right[carrier : carrier + 1]
    speed = jnp.maximum(jnp.abs(a_left), jnp.abs(a_right))
    return 0.5 * (a_left * left + a_right * right) - 0.5 * speed * (right - left)


def lon_divergence(row):
    size = row.shape[2]
    jump = pltpu.roll(row, size - 1, 2) - row
    half = 0.5 * minmod(pltpu.roll(jump, 1, 2), jump)
    flux = upwind(row + half, pltpu.roll(row - half, size - 1, 2), 0)
    return flux - pltpu.roll(flux, 1, 2)


def advance_rows(load, store, count):
    rows = [load(i) for i in range(4)]
    jumps = [rows[i + 1] - rows[i] for i in range(3)]
    halves = [0.5 * minmod(jumps[i], jumps[i + 1]) for i in range(2)]
    lower = upwind(rows[1] + halves[0], rows[2] - halves[1], 1)
    for k in range(count):
        ahead = load(k + 4)
        jump = ahead - rows[3]
        half = 0.5 * minmod(jumps[2], jump)
        upper = upwind(rows[2] + halves[1], rows[3] - half, 1)
        centre = rows[2]
        store(k, centre - COURANT * ((upper - lower) + lon_divergence(centre)))
        rows = rows[1:] + [ahead]
        jumps = jumps[1:] + [jump]
        halves = [halves[1], half]
        lower = upper


def cycle_kernel(
    bands,
    mems,
    loc_ref,
    near_ref,
    x_ref,
    value_ref,
    site_ref,
    count_ref,
    precision_ref,
    out_ref,
    first,
    second,
    third,
    state,
    weight_buf,
    target_buf,
    anomaly,
    means,
    gram,
    pull,
    root,
    inverse,
    turned,
    result,
    final,
    send_a,
    recv_a,
    send_b,
    recv_b,
    send_d,
    recv_d,
    local_sem,
):
    band = lax.axis_index("band")
    mem = lax.axis_index("mem")
    side = lax.rem(band, 2)
    base = band - side
    nv, lat, group, lon = x_ref.shape
    half = group // 2
    tiles = lon // TILE
    members = group * mems
    sites = nv * TILE
    me = side * mems + mem

    def greet(b, m, okay):
        @pl.when(okay)
        def _():
            pl.semaphore_signal(
                barrier, inc=1, device_id={"band": b, "mem": m}, device_id_type=MESH
            )

        return okay.astype(jnp.int32) if hasattr(okay, "astype") else jnp.int32(okay)

    barrier = pltpu.get_barrier_semaphore()
    partners = jnp.int32(0)
    for k in range(2 * mems):
        partners += greet(base + k // mems, jnp.int32(k % mems), me != k)
    near_band = jnp.where(side == 0, base - 1, base + 2)
    near_okay = (near_band >= 0) & (near_band < bands)
    for m in range(mems):
        partners += greet(near_band, jnp.int32(m), near_okay)
    past_band = jnp.where(side == 0, base - 2, base + 3)
    partners += greet(past_band, mem, near_okay)
    other_band = jnp.where(side == 0, base + 2, base - 1)
    other_okay = (other_band >= 0) & (other_band < bands)
    partners += greet(other_band, mem, other_okay)
    pl.semaphore_wait(barrier, partners)

    def part(h):
        return x_ref.at[:, :, pl.ds(h * half, half), :]

    def slot(k):
        return first.at[:, pl.ds(k * lat, lat), :, :]

    def copy_a(h, place, sem, target):
        return pltpu.make_async_remote_copy(
            src_ref=part(h),
            dst_ref=slot(place),
            send_sem=send_a.at[sem],
            recv_sem=recv_a.at[place],
            device_id={"band": target, "mem": mem},
            device_id_type=MESH,
        )

    own_a = pltpu.make_async_copy(part(side), slot(1 + side), local_sem.at[0])
    far_place = 3 - 3 * side
    far_base = base - 2 + 4 * side
    to_pair = copy_a(1 - side, 1 + side, 0, base + 1 - side)
    to_far = [copy_a(h, far_place, 1 + h, far_base + h) for h in range(2)]

    @pl.when(near_okay)
    def _():
        for copy in to_far:
            copy.start()

    to_pair.start()
    own_a.start()

    zeros = jnp.zeros((nv, lat, half, lon), jnp.float32)

    @pl.when(base == 0)
    def _():
        first[:, 0:lat] = zeros

    @pl.when(base == bands - 2)
    def _():
        first[:, 3 * lat : 4 * lat] = zeros

    slots = value_ref.shape[1]
    live = lax.broadcasted_iota(jnp.int32, (tiles, slots), 1) < count_ref[...]
    precision = jnp.where(live, precision_ref[...], 0.0)
    weighted_value = precision * value_ref[...]
    site_index = lax.broadcasted_iota(jnp.int32, (sites, slots), 0)
    for u in range(tiles):
        match = site_index == site_ref[u : u + 1, :]
        total = jnp.sum(jnp.where(match, precision[u : u + 1, :], 0.0), axis=1, keepdims=True)
        weight_buf[u] = jnp.broadcast_to(total, (sites, members))
        total = jnp.sum(jnp.where(match, weighted_value[u : u + 1, :], 0.0), axis=1, keepdims=True)
        target_buf[u] = jnp.broadcast_to(total, (sites, members))

    own_a.wait()
    to_pair.wait_send()
    copy_a(side, 2 - side, 0, base + 1 - side).wait_recv()

    @pl.when(base > 0)
    def _():
        copy_a(side, 0, 0, base + 1 - side).wait_recv()

    @pl.when(base < bands - 2)
    def _():
        copy_a(side, 3, 0, base + 1 - side).wait_recv()

    @pl.when(near_okay)
    def _():
        for copy in to_far:
            copy.wait_send()

    edge = 2
    low_mask = jnp.where(base > 0, 1.0, 0.0)
    high_mask = jnp.where(base < bands - 2, 1.0, 0.0)

    def store_second(k, row):
        if k < lat - edge:
            row = row * low_mask
        if k >= 3 * lat - edge:
            row = row * high_mask
        second[k] = row

    advance_rows(lambda i: first[:, i], store_second, 4 * lat - 2 * edge)

    def copy_b(k, sender):
        return pltpu.make_async_remote_copy(
            src_ref=third.at[k],
            dst_ref=state.at[sender],
            send_sem=send_b.at[k],
            recv_sem=recv_b.at[sender],
            device_id={"band": base + k // mems, "mem": jnp.int32(k % mems)},
            device_id_type=MESH,
        )

    def store_third(k, row):
        third[k] = row

        @pl.when(me != k)
        def _():
            copy_b(k, me).start()

        @pl.when(me == k)
        def _():
            state[me] = row

    advance_rows(lambda i: second[i], store_third, 2 * lat)

    for k in range(2 * mems):

        @pl.when(me != k)
        def _():
            copy_b(k, jnp.int32(k)).wait_recv()

    for v in range(nv):
        parts = [state[(k % 2) * mems + k // 2, v] for k in range(2 * mems)]
        field = jnp.concatenate(parts, axis=0).T
        mean = jnp.mean(field, axis=1, keepdims=True)
        means[v] = jnp.broadcast_to(mean, (lon, members))
        anomaly[v] = field - mean

    def of_tile(ref, u):
        return jnp.concatenate([ref[v, u * TILE : (u + 1) * TILE, :] for v in range(nv)], axis=0)

    for u in range(tiles):
        p = of_tile(anomaly, u)
        d = weight_buf[u]
        p_high, p_low = split_pair(p)
        w_high, w_low = split_pair(p * d)
        gram[u] = lax.dot_general(
            jnp.concatenate([w_high, w_low, w_high], axis=0),
            jnp.concatenate([p_high, p_high, p_low], axis=0),
            (((0,), (0,)), ((), ())),
            preferred_element_type=jnp.float32,
        )
        pull[u] = jnp.sum(p * (target_buf[u] - d * of_tile(means, u)), axis=0, keepdims=True)

    identity = (
        lax.broadcasted_iota(jnp.int32, (members, members), 0)
        == lax.broadcasted_iota(jnp.int32, (members, members), 1)
    ).astype(jnp.float32)
    listed = near_ref.shape[1]
    norms = []
    drives = []
    for t in range(tiles):
        a = (members - 1.0) * identity
        drive = jnp.zeros((1, members), jnp.float32)
        for j in range(listed):
            u = near_ref[t, j]
            scale = loc_ref[t, j]
            a += scale * gram[u]
            drive += scale * pull[u]
        norm = jnp.sqrt(jnp.sum(jnp.sum(a * a, axis=1, keepdims=True), axis=0, keepdims=True))
        norms.append(norm)
        drives.append(drive)
        r = a * (1.0 / norm)
        s = 1.5 * identity - 0.5 * r
        root[t] = pair_dot(left_form(r), right_form(s))
        inverse[t] = s

    def sweep(_, carry):
        for t in range(tiles):
            r, z = root[t], inverse[t]
            r_left, r_right = left_form(r), right_form(r)
            s = 1.5 * identity - 0.5 * pair_dot(left_form(z), r_right)
            root[t] = pair_dot(r_left, right_form(s))
            inverse[t] = pair_dot(left_form(s), right_form(z))
        return carry

    lax.fori_loop(0, NSI - 2, sweep, 0)

    for t in range(tiles):
        r, z = root[t], inverse[t]
        s = 1.5 * identity - 0.5 * pair_dot(left_form(z), right_form(r))
        z = pair_dot(left_form(s), right_form(z))
        p = of_tile(anomaly, t)
        stacked = jnp.concatenate(
            [p, jnp.broadcast_to(drives[t], (TILE, members))], axis=0
        )
        applied = pair_dot(left_form(stacked), right_form(z))
        q = applied[:sites]
        step = applied[sites : sites + 1]
        shift = jnp.sum(q * step, axis=1, keepdims=True) / norms[t]
        new = of_tile(means, t) + q * jnp.sqrt((members - 1.0) / norms[t]) + shift
        for v in range(nv):
            turned[v, t * TILE : (t + 1) * TILE, :] = new[v * TILE : (v + 1) * TILE, :]

    for v in range(nv):
        result[v] = turned[v].T

    def copy_d(m, place, sem, target):
        return pltpu.make_async_remote_copy(
            src_ref=result.at[:, pl.ds(m * group, group), :],
            dst_ref=final.at[place],
            send_sem=send_d.at[sem],
            recv_sem=recv_d.at[place],
            device_id={"band": target, "mem": jnp.int32(m)},
            device_id_type=MESH,
        )

    outward = 1 - 2 * (mem < edge).astype(jnp.int32)
    out_band = band + outward
    out_okay = (out_band >= 0) & (out_band < bands)
    out_place = mem + edge - outward * lat
    for m in range(mems):

        @pl.when(out_okay)
        def _():
            copy_d(m, out_place, mems + m, out_band).start()

    for m in range(mems):

        @pl.when(mem != m)
        def _():
            copy_d(m, mem + edge, m, band).start()

    own_d = pltpu.make_async_copy(
        result.at[:, pl.ds(mem * group, group), :], final.at[mem + edge], local_sem.at[1]
    )
    own_d.start()

    blank = jnp.zeros((edge, nv, group, lon), jnp.float32)

    @pl.when(band == 0)
    def _():
        final[0:edge] = blank

    @pl.when(band == bands - 1)
    def _():
        final[lat + edge : lat + 2 * edge] = blank

    own_d.wait()
    for k in range(lat + 2 * edge):
        if k < edge:
            okay = band > 0
        elif k < lat + edge:
            okay = mem != k - edge
        else:
            okay = band < bands - 1

        @pl.when(okay)
        def _():
            copy_d(0, k, 0, band).wait_recv()

    def store_out(k, row):
        out_ref[k] = row

    advance_rows(lambda i: final[i], store_out, lat)

    for k in range(2 * mems):

        @pl.when(me != k)
        def _():
            copy_b(k, me).wait_send()

    for m in range(mems):

        @pl.when(out_okay)
        def _():
            copy_d(m, out_place, mems + m, out_band).wait_send()

        @pl.when(mem != m)
        def _():
            copy_d(m, mem + edge, m, band).wait_send()


def fused_shards(
    bands, mems, ensemble, obs_value, obs_site, obs_count, obs_precision, loc_weight, neighbours
):
    group, nv, lat, lon = ensemble.shape
    half = group // 2
    tiles = lon // TILE
    members = group * mems
    sites = nv * TILE
    edge = 2
    f32 = jnp.float32
    vmem = pl.BlockSpec(memory_space=pltpu.VMEM)
    smem = pl.BlockSpec(memory_space=pltpu.SMEM)
    rows = pl.pallas_call(
        functools.partial(cycle_kernel, bands, mems),
        out_shape=jax.ShapeDtypeStruct((lat, nv, group, lon), f32),
        in_specs=[smem, smem] + [vmem] * 5,
        out_specs=vmem,
        scratch_shapes=[
            pltpu.VMEM((nv, 4 * lat, half, lon), f32),
            pltpu.VMEM((4 * lat - 2 * edge, nv, half, lon), f32),
            pltpu.VMEM((2 * lat, nv, half, lon), f32),
            pltpu.VMEM((2 * mems, nv, half, lon), f32),
            pltpu.VMEM((tiles, sites, members), f32),
            pltpu.VMEM((tiles, sites, members), f32),
            pltpu.VMEM((nv, lon, members), f32),
            pltpu.VMEM((nv, lon, members), f32),
            pltpu.VMEM((tiles, members, members), f32),
            pltpu.VMEM((tiles, 1, members), f32),
            pltpu.VMEM((tiles, members, members), f32),
            pltpu.VMEM((tiles, members, members), f32),
            pltpu.VMEM((nv, lon, members), f32),
            pltpu.VMEM((nv, members, lon), f32),
            pltpu.VMEM((lat + 2 * edge, nv, group, lon), f32),
            pltpu.SemaphoreType.DMA((3,)),
            pltpu.SemaphoreType.DMA((4,)),
            pltpu.SemaphoreType.DMA((2 * mems,)),
            pltpu.SemaphoreType.DMA((2 * mems,)),
            pltpu.SemaphoreType.DMA((2 * mems,)),
            pltpu.SemaphoreType.DMA((lat + 2 * edge,)),
            pltpu.SemaphoreType.DMA((2,)),
        ],
        compiler_params=pltpu.CompilerParams(collective_id=0, has_side_effects=True),
    )(
        loc_weight,
        neighbours,
        ensemble.transpose(1, 2, 0, 3),
        obs_value,
        obs_site,
        obs_count[:, None],
        obs_precision,
    )
    return rows.transpose(2, 1, 0, 3)


def solution(mesh):
    bands, mems = mesh.shape["band"], mesh.shape["mem"]

    def body(ensemble, *rest):
        group, _, lat, lon = ensemble.shape
        fits = (
            STEPS == 2
            and lat == 4
            and lat == mems
            and bands % 2 == 0
            and group % 16 == 0
            and lon == group * mems == 128
        )
        if fits:
            return fused_shards(bands, mems, ensemble, *rest)
        return shards(ensemble, *rest)

    return jax.shard_map(
        body,
        mesh=mesh,
        in_specs=(
            P("mem", None, "band", None),
            P(("band", "mem"), None),
            P(("band", "mem"), None),
            P(("band", "mem")),
            P(("band", "mem"), None),
            P(("band", "mem"), None),
            P(("band", "mem"), None),
        ),
        out_specs=P("mem", None, "band", None),
        check_vma=False,
    )
```

```python
import functools

import jax
import jax.numpy as jnp
from jax import lax
from jax.experimental import pallas as pl
from jax.experimental.pallas import tpu as pltpu
from jax.sharding import PartitionSpec as P

TILE = 16
NSI = 6
STEPS = 2


COURANT = 0.08
HIGHEST = lax.Precision.HIGHEST
MESH = pl.DeviceIdType.MESH


def extended_2(block, sides, width):
    for axis, dim in sides:
        count = lax.axis_size(axis)
        forward = [(i, i + 1) for i in range(count - 1)]
        backward = [(target, source) for source, target in forward]
        low = lax.ppermute(
            lax.slice_in_dim(block, block.shape[dim] - width, None, axis=dim), axis, forward
        )
        high = lax.ppermute(lax.slice_in_dim(block, 0, width, axis=dim), axis, backward)
        block = jnp.concatenate([low, block, high], axis=dim)
    return block


def minmod(lower_jump, upper_jump):
    return jnp.maximum(0.0, jnp.minimum(lower_jump, upper_jump)) + jnp.minimum(
        0.0, jnp.maximum(lower_jump, upper_jump)
    )


def flux_divergence(halo_extended_field, sweep_direction, advected_field):
    extent = halo_extended_field.shape[sweep_direction]
    differences = lax.slice_in_dim(
        halo_extended_field, 1, extent, axis=sweep_direction
    ) - lax.slice_in_dim(halo_extended_field, 0, extent - 1, axis=sweep_direction)
    slopes = minmod(
        lax.slice_in_dim(differences, 0, extent - 2, axis=sweep_direction),
        lax.slice_in_dim(differences, 1, extent - 1, axis=sweep_direction),
    )
    state_left_side = lax.slice_in_dim(
        halo_extended_field, 1, extent - 2, axis=sweep_direction
    ) + 0.5 * lax.slice_in_dim(slopes, 0, extent - 3, axis=sweep_direction)
    state_right_side = lax.slice_in_dim(
        halo_extended_field, 2, extent - 1, axis=sweep_direction
    ) - 0.5 * lax.slice_in_dim(slopes, 1, extent - 2, axis=sweep_direction)
    advected_field_left = state_left_side[:, advected_field : advected_field + 1]
    advected_field_right = state_right_side[:, advected_field : advected_field + 1]
    signal_velocity = jnp.maximum(jnp.abs(advected_field_left), jnp.abs(advected_field_right))
    interface_fluxes = 0.5 * (
        advected_field_left * state_left_side + advected_field_right * state_right_side
    ) - 0.5 * signal_velocity * (state_right_side - state_left_side)
    return lax.slice_in_dim(
        interface_fluxes, 1, extent - 3, axis=sweep_direction
    ) - lax.slice_in_dim(interface_fluxes, 0, extent - 4, axis=sweep_direction)


def advance(halo_extended_field):
    centre = halo_extended_field[:, :, 2:-2]
    lat_div = flux_divergence(halo_extended_field, 2, 1)
    wrapped = jnp.concatenate([centre[..., -2:], centre, centre[..., :2]], axis=3)
    lon_div = flux_divergence(wrapped, 3, 0)
    return centre - COURANT * (lat_div + lon_div)


def obs_space(tile_state, obs_value, obs_site):
    site_count = tile_state.shape[2]
    ens_mean = jnp.mean(tile_state, axis=1)
    anomaly = tile_state - ens_mean[:, None, :]
    selector = (obs_site[:, :, None] == jnp.arange(site_count)[None, None, :]).astype(jnp.float32)
    obs_anomaly = jnp.einsum("bos,bks->bok", selector, anomaly, precision=HIGHEST)
    obs_mean = jnp.einsum("bos,bs->bo", selector, ens_mean, precision=HIGHEST)
    return (ens_mean, anomaly, obs_anomaly, obs_value - obs_mean)


def transform(local_anomaly, local_innovation, local_weight, ens_mean, anomaly):
    members = local_anomaly.shape[2]
    identity = jnp.eye(members, dtype=jnp.float32)
    weighted = local_anomaly * local_weight[:, :, None]
    gram_matrix = (
        jnp.einsum("bpk,bpj->bkj", weighted, local_anomaly, precision=HIGHEST)
        + (members - 1.0) * identity
    )
    frob_norm = jnp.sqrt(jnp.sum(gram_matrix * gram_matrix, axis=(1, 2)))
    root_iter = gram_matrix / frob_norm[:, None, None]
    inverse = jnp.broadcast_to(identity, gram_matrix.shape)
    for sweep in range(NSI):
        factor = 1.5 * identity - 0.5 * jnp.matmul(inverse, root_iter, precision=HIGHEST)
        root_iter = jnp.matmul(root_iter, factor, precision=HIGHEST)
        inverse = jnp.matmul(factor, inverse, precision=HIGHEST)
    projected = jnp.einsum("bpk,bp->bk", weighted, local_innovation, precision=HIGHEST)
    halfway = jnp.einsum("bkj,bj->bk", inverse, projected, precision=HIGHEST)
    mean_weights = (
        jnp.einsum("bkj,bj->bk", inverse, halfway, precision=HIGHEST) / frob_norm[:, None]
    )
    spread_weights = inverse * jnp.sqrt((members - 1.0) / frob_norm)[:, None, None]
    combined = spread_weights + mean_weights[:, :, None]
    return ens_mean[:, None, :] + jnp.einsum("bjk,bjs->bks", combined, anomaly, precision=HIGHEST)


def localise(obs_anomaly, innovation, slot_weight, neighbour_tiles, loc_weight, ens_mean, anomaly):
    batch_tiles = neighbour_tiles.shape[0]
    local_anomaly = obs_anomaly[neighbour_tiles].reshape(batch_tiles, -1, obs_anomaly.shape[2])
    local_innovation = innovation[neighbour_tiles].reshape(batch_tiles, -1)
    local_weight = (loc_weight[:, :, None] * slot_weight[neighbour_tiles]).reshape(batch_tiles, -1)
    return transform(local_anomaly, local_innovation, local_weight, ens_mean, anomaly)


def shards(ensemble, obs_value, obs_site, obs_count, obs_precision, loc_weight, neighbours):
    fields = ensemble
    lat_rows = fields.shape[2]
    margin = 2 * STEPS
    extended = extended_2(fields, (("band", 2),), margin)
    offset = lax.axis_index("band") * lat_rows
    lat_total = lat_rows * lax.axis_size("band")
    for repeat in range(STEPS):
        extended = advance(extended)
        remaining = margin - 2 * (repeat + 1)
        if remaining > 0:
            global_row = (
                lax.broadcasted_iota(jnp.int32, (1, 1, extended.shape[2], 1), 2)
                - remaining
                + offset
            )
            inside = (global_row >= 0) & (global_row < lat_total)
            extended = jnp.where(inside, extended, 0.0)
    fields = extended
    members, variables, lon_total = (fields.shape[0], fields.shape[1], fields.shape[3])
    flattened = fields.reshape(members, variables, lat_rows * lon_total)
    grouped = lax.all_to_all(flattened, "mem", split_axis=2, concat_axis=0, tiled=True)
    all_members = grouped.shape[0]
    tile_count = neighbours.shape[0]
    tile_state = (
        grouped.reshape(all_members, variables, tile_count, TILE)
        .transpose(2, 0, 1, 3)
        .reshape(tile_count, all_members, variables * TILE)
    )
    ens_mean, anomaly, obs_anomaly, innovation = obs_space(tile_state, obs_value, obs_site)
    live_slots = jnp.arange(obs_value.shape[1])[None, :] < obs_count[:, None]
    slot_weight = jnp.where(live_slots, obs_precision, 0.0)
    analysed = localise(
        obs_anomaly, innovation, slot_weight, neighbours, loc_weight, ens_mean, anomaly
    )
    outgoing = (
        analysed.reshape(tile_count, all_members, variables, TILE)
        .transpose(1, 2, 0, 3)
        .reshape(all_members, variables, tile_count * TILE)
    )
    returned = lax.all_to_all(outgoing, "mem", split_axis=0, concat_axis=2, tiled=True)
    fields = returned.reshape(members, variables, lat_rows, lon_total)
    return advance(extended_2(fields, (("band", 2),), 2))


def split_pair(x):
    high = x.astype(jnp.bfloat16)
    low = (x - high.astype(jnp.float32)).astype(jnp.bfloat16)
    return high, low


def left_form(x):
    return jnp.concatenate(split_pair(x), axis=1)


def right_form(x):
    wide = jnp.concatenate(split_pair(x), axis=1)
    return jnp.concatenate([wide, wide], axis=0)


def pair_dot(left, right):
    both = jnp.dot(left, right, preferred_element_type=jnp.float32)
    half = both.shape[1] // 2
    return both[:, :half] + both[:, half:]


def upwind(left, right, carrier):
    a_left = left[carrier : carrier + 1]
    a_right = right[carrier : carrier + 1]
    speed = jnp.maximum(jnp.abs(a_left), jnp.abs(a_right))
    return 0.5 * (a_left * left + a_right * right) - 0.5 * speed * (right - left)


def lon_divergence(row):
    size = row.shape[2]
    jump = pltpu.roll(row, size - 1, 2) - row
    half = 0.5 * minmod(pltpu.roll(jump, 1, 2), jump)
    flux = upwind(row + half, pltpu.roll(row - half, size - 1, 2), 0)
    return flux - pltpu.roll(flux, 1, 2)


def advance_rows(load, store, count):
    rows = [load(i) for i in range(4)]
    jumps = [rows[i + 1] - rows[i] for i in range(3)]
    halves = [0.5 * minmod(jumps[i], jumps[i + 1]) for i in range(2)]
    lower = upwind(rows[1] + halves[0], rows[2] - halves[1], 1)
    for k in range(count):
        ahead = load(k + 4)
        jump = ahead - rows[3]
        half = 0.5 * minmod(jumps[2], jump)
        upper = upwind(rows[2] + halves[1], rows[3] - half, 1)
        centre = rows[2]
        store(k, centre - COURANT * ((upper - lower) + lon_divergence(centre)))
        rows = rows[1:] + [ahead]
        jumps = jumps[1:] + [jump]
        halves = [halves[1], half]
        lower = upper


def cycle_kernel(
    bands,
    mems,
    loc_ref,
    near_ref,
    count_ref,
    x_ref,
    value_ref,
    site_ref,
    precision_ref,
    out_ref,
    first,
    second,
    third,
    state,
    weight_buf,
    target_buf,
    anomaly,
    means,
    gram,
    pull,
    root,
    inverse,
    turned,
    result,
    final,
    send_a,
    recv_a,
    send_b,
    recv_b,
    send_d,
    recv_d,
    local_sem,
):
    band = lax.axis_index("band")
    mem = lax.axis_index("mem")
    side = lax.rem(band, 2)
    base = band - side
    lon = x_ref.shape[1]
    half = state.shape[2]
    group = 2 * half
    nv = state.shape[1]
    lat = x_ref.shape[0] // (group * nv)
    span = nv * lat
    tiles = lon // TILE
    members = group * mems
    sites = nv * TILE
    me = side * mems + mem

    def greet(b, m, okay):
        @pl.when(okay)
        def _():
            pl.semaphore_signal(
                barrier, inc=1, device_id={"band": b, "mem": m}, device_id_type=MESH
            )

        return okay.astype(jnp.int32) if hasattr(okay, "astype") else jnp.int32(okay)

    barrier = pltpu.get_barrier_semaphore()
    partners = jnp.int32(0)
    for k in range(2 * mems):
        partners += greet(base + k // mems, jnp.int32(k % mems), me != k)
    near_band = jnp.where(side == 0, base - 1, base + 2)
    near_okay = (near_band >= 0) & (near_band < bands)
    for m in range(mems):
        partners += greet(near_band, jnp.int32(m), near_okay)
    past_band = jnp.where(side == 0, base - 2, base + 3)
    partners += greet(past_band, mem, near_okay)
    other_band = jnp.where(side == 0, base + 2, base - 1)
    other_okay = (other_band >= 0) & (other_band < bands)
    partners += greet(other_band, mem, other_okay)
    slots = value_ref.shape[1]
    slot_index = lax.broadcasted_iota(jnp.int32, (1, slots), 1)
    site_index = lax.broadcasted_iota(jnp.int32, (sites, slots), 0)
    for u in range(tiles):
        match = site_index == site_ref[u : u + 1, :]
        live = slot_index < count_ref[0, u]
        precision = jnp.where(live, precision_ref[u : u + 1, :], 0.0)
        weighted_value = precision * value_ref[u : u + 1, :]
        total = jnp.sum(jnp.where(match, precision, 0.0), axis=1, keepdims=True)
        weight_buf[u] = jnp.broadcast_to(total, (sites, members))
        total = jnp.sum(jnp.where(match, weighted_value, 0.0), axis=1, keepdims=True)
        target_buf[u] = jnp.broadcast_to(total, (sites, members))

    pl.semaphore_wait(barrier, partners)

    chunks = 4
    depth = half * span // chunks

    def copy_a(src, place, c, sem, target):
        return pltpu.make_async_remote_copy(
            src_ref=src,
            dst_ref=first.at[place, pl.ds(c * depth, depth), :],
            send_sem=send_a.at[sem, c],
            recv_sem=recv_a.at[place, c],
            device_id={"band": target, "mem": mem},
            device_id_type=MESH,
        )

    def own_part(h, c):
        return x_ref.at[pl.ds(h * half * span + c * depth, depth), :]

    own_a = pltpu.make_async_copy(
        x_ref.at[pl.ds(side * half * span, half * span), :], first.at[1 + side], local_sem.at[0]
    )
    partner = base + 1 - side
    got = 2 - side
    to_pair = [copy_a(own_part(1 - side, c), 1 + side, c, 0, partner) for c in range(chunks)]
    to_past = [copy_a(own_part(side, c), 3 - 3 * side, c, 1, past_band) for c in range(chunks)]
    relayed = [
        copy_a(first.at[got, pl.ds(c * depth, depth), :], 3 * side, c, 2, other_band)
        for c in range(chunks)
    ]

    for copy in to_pair:
        copy.start()

    @pl.when(near_okay)
    def _():
        for copy in to_past:
            copy.start()

    own_a.start()

    zeros = jnp.zeros((half * span, lon), jnp.float32)

    @pl.when(base == 0)
    def _():
        first[0] = zeros

    @pl.when(base == bands - 2)
    def _():
        first[3] = zeros

    def arrive(place, c):
        copy_a(own_part(side, c), place, c, 0, partner).wait_recv()

    for c in range(chunks):
        arrive(got, c)

        @pl.when(other_okay)
        def _():
            relayed[c].start()

    own_a.wait()

    @pl.when(base > 0)
    def _():
        for c in range(chunks):
            arrive(0, c)

    @pl.when(base < bands - 2)
    def _():
        for c in range(chunks):
            arrive(3, c)

    edge = 2
    low_mask = jnp.where(base > 0, 1.0, 0.0)
    high_mask = jnp.where(base < bands - 2, 1.0, 0.0)

    def store_second(k, row):
        if k < lat - edge:
            row = row * low_mask
        if k >= 3 * lat - edge:
            row = row * high_mask
        second[k] = row

    def load_first(i):
        return jnp.stack(
            [first[i // lat, pl.ds(v * lat + i % lat, half, stride=span), :] for v in range(nv)]
        )

    advance_rows(load_first, store_second, 4 * lat - 2 * edge)

    def copy_b(k, sender):
        return pltpu.make_async_remote_copy(
            src_ref=third.at[k],
            dst_ref=state.at[sender],
            send_sem=send_b.at[k],
            recv_sem=recv_b.at[sender],
            device_id={"band": base + k // mems, "mem": jnp.int32(k % mems)},
            device_id_type=MESH,
        )

    def store_third(k, row):
        third[k] = row

        @pl.when(me != k)
        def _():
            copy_b(k, me).start()

        @pl.when(me == k)
        def _():
            state[me] = row

    advance_rows(lambda i: second[i], store_third, 2 * lat)

    for k in range(2 * mems):

        @pl.when(me != k)
        def _():
            copy_b(k, jnp.int32(k)).wait_recv()

    for v in range(nv):
        parts = [state[(k % 2) * mems + k // 2, v] for k in range(2 * mems)]
        field = jnp.concatenate(parts, axis=0).T
        mean = jnp.mean(field, axis=1, keepdims=True)
        means[v] = jnp.broadcast_to(mean, (lon, members))
        anomaly[v] = field - mean

    def of_tile(ref, u):
        return jnp.concatenate([ref[v, u * TILE : (u + 1) * TILE, :] for v in range(nv)], axis=0)

    for u in range(tiles):
        p = of_tile(anomaly, u)
        d = weight_buf[u]
        p_high, p_low = split_pair(p)
        w_high, w_low = split_pair(p * d)
        gram[u] = lax.dot_general(
            jnp.concatenate([w_high, w_low, w_high], axis=0),
            jnp.concatenate([p_high, p_high, p_low], axis=0),
            (((0,), (0,)), ((), ())),
            preferred_element_type=jnp.float32,
        )
        pull[u] = jnp.sum(p * (target_buf[u] - d * of_tile(means, u)), axis=0, keepdims=True)

    identity = (
        lax.broadcasted_iota(jnp.int32, (members, members), 0)
        == lax.broadcasted_iota(jnp.int32, (members, members), 1)
    ).astype(jnp.float32)
    listed = near_ref.shape[0]
    norms = []
    drives = []
    for t in range(tiles):
        a = (members - 1.0) * identity
        drive = jnp.zeros((1, members), jnp.float32)
        for j in range(listed):
            u = near_ref[j, t]
            scale = loc_ref[j, t]
            a += scale * gram[u]
            drive += scale * pull[u]
        norm = jnp.sqrt(jnp.sum(jnp.sum(a * a, axis=1, keepdims=True), axis=0, keepdims=True))
        norms.append(norm)
        drives.append(drive)
        r = a * (1.0 / norm)
        s = 1.5 * identity - 0.5 * r
        root[t] = pair_dot(left_form(r), right_form(s))
        inverse[t] = s

    def sweep(_, carry):
        for t in range(tiles):
            r, z = root[t], inverse[t]
            r_left, r_right = left_form(r), right_form(r)
            s = 1.5 * identity - 0.5 * pair_dot(left_form(z), r_right)
            root[t] = pair_dot(r_left, right_form(s))
            inverse[t] = pair_dot(left_form(s), right_form(z))
        return carry

    lax.fori_loop(0, NSI - 2, sweep, 0)

    for t in range(tiles):
        r, z = root[t], inverse[t]
        s = 1.5 * identity - 0.5 * pair_dot(left_form(z), right_form(r))
        z = pair_dot(left_form(s), right_form(z))
        p = of_tile(anomaly, t)
        stacked = jnp.concatenate(
            [p, jnp.broadcast_to(drives[t], (TILE, members))], axis=0
        )
        applied = pair_dot(left_form(stacked), right_form(z))
        q = applied[:sites]
        step = applied[sites : sites + 1]
        shift = jnp.sum(q * step, axis=1, keepdims=True) / norms[t]
        new = of_tile(means, t) + q * jnp.sqrt((members - 1.0) / norms[t]) + shift
        for v in range(nv):
            turned[v, t * TILE : (t + 1) * TILE, :] = new[v * TILE : (v + 1) * TILE, :]

    for v in range(nv):
        result[v] = turned[v].T

    def copy_d(m, place, sem, target):
        return pltpu.make_async_remote_copy(
            src_ref=result.at[:, pl.ds(m * group, group), :],
            dst_ref=final.at[place],
            send_sem=send_d.at[sem],
            recv_sem=recv_d.at[place],
            device_id={"band": target, "mem": jnp.int32(m)},
            device_id_type=MESH,
        )

    outward = 1 - 2 * (mem < edge).astype(jnp.int32)
    out_band = band + outward
    out_okay = (out_band >= 0) & (out_band < bands)
    out_place = mem + edge - outward * lat
    for m in range(mems):

        @pl.when(out_okay)
        def _():
            copy_d(m, out_place, mems + m, out_band).start()

    for m in range(mems):

        @pl.when(mem != m)
        def _():
            copy_d(m, mem + edge, m, band).start()

    own_d = pltpu.make_async_copy(
        result.at[:, pl.ds(mem * group, group), :], final.at[mem + edge], local_sem.at[1]
    )
    own_d.start()

    blank = jnp.zeros((edge, nv, group, lon), jnp.float32)

    @pl.when(band == 0)
    def _():
        final[0:edge] = blank

    @pl.when(band == bands - 1)
    def _():
        final[lat + edge : lat + 2 * edge] = blank

    own_d.wait()
    for k in range(lat + 2 * edge):
        if k < edge:
            okay = band > 0
        elif k < lat + edge:
            okay = mem != k - edge
        else:
            okay = band < bands - 1

        @pl.when(okay)
        def _():
            copy_d(0, k, 0, band).wait_recv()

    def store_out(k, row):
        for v in range(nv):
            out_ref[pl.ds(v * lat + k, group, stride=span), :] = row[v]

    advance_rows(lambda i: final[i], store_out, lat)

    for copy in to_pair:
        copy.wait_send()

    @pl.when(near_okay)
    def _():
        for copy in to_past:
            copy.wait_send()

    @pl.when(other_okay)
    def _():
        for copy in relayed:
            copy.wait_send()

    for k in range(2 * mems):

        @pl.when(me != k)
        def _():
            copy_b(k, me).wait_send()

    for m in range(mems):

        @pl.when(out_okay)
        def _():
            copy_d(m, out_place, mems + m, out_band).wait_send()

        @pl.when(mem != m)
        def _():
            copy_d(m, mem + edge, m, band).wait_send()


def fused_shards(
    bands, mems, ensemble, obs_value, obs_site, obs_count, obs_precision, loc_weight, neighbours
):
    group, nv, lat, lon = ensemble.shape
    half = group // 2
    tiles = lon // TILE
    members = group * mems
    sites = nv * TILE
    edge = 2
    f32 = jnp.float32
    vmem = pl.BlockSpec(memory_space=pltpu.VMEM)
    smem = pl.BlockSpec(memory_space=pltpu.SMEM)
    rows = pl.pallas_call(
        functools.partial(cycle_kernel, bands, mems),
        out_shape=jax.ShapeDtypeStruct((group * nv * lat, lon), f32),
        in_specs=[smem] * 3 + [pl.BlockSpec(memory_space=pl.ANY)] + [vmem] * 3,
        out_specs=vmem,
        scratch_shapes=[
            pltpu.VMEM((4, half * nv * lat, lon), f32),
            pltpu.VMEM((4 * lat - 2 * edge, nv, half, lon), f32),
            pltpu.VMEM((2 * lat, nv, half, lon), f32),
            pltpu.VMEM((2 * mems, nv, half, lon), f32),
            pltpu.VMEM((tiles, sites, members), f32),
            pltpu.VMEM((tiles, sites, members), f32),
            pltpu.VMEM((nv, lon, members), f32),
            pltpu.VMEM((nv, lon, members), f32),
            pltpu.VMEM((tiles, members, members), f32),
            pltpu.VMEM((tiles, 1, members), f32),
            pltpu.VMEM((tiles, members, members), f32),
            pltpu.VMEM((tiles, members, members), f32),
            pltpu.VMEM((nv, lon, members), f32),
            pltpu.VMEM((nv, members, lon), f32),
            pltpu.VMEM((lat + 2 * edge, nv, group, lon), f32),
            pltpu.SemaphoreType.DMA((3, 4)),
            pltpu.SemaphoreType.DMA((4, 4)),
            pltpu.SemaphoreType.DMA((2 * mems,)),
            pltpu.SemaphoreType.DMA((2 * mems,)),
            pltpu.SemaphoreType.DMA((2 * mems,)),
            pltpu.SemaphoreType.DMA((lat + 2 * edge,)),
            pltpu.SemaphoreType.DMA((2,)),
        ],
        compiler_params=pltpu.CompilerParams(collective_id=0, has_side_effects=True),
    )(
        loc_weight.T,
        neighbours.T,
        obs_count[None, :],
        ensemble.reshape(group * nv * lat, lon),
        obs_value,
        obs_site,
        obs_precision,
    )
    return rows.reshape(ensemble.shape)


def solution(mesh):
    bands, mems = mesh.shape["band"], mesh.shape["mem"]

    def body(ensemble, *rest):
        group, _, lat, lon = ensemble.shape
        fits = (
            STEPS == 2
            and lat == 4
            and lat == mems
            and bands % 2 == 0
            and group % 16 == 0
            and lon == group * mems == 128
        )
        if fits:
            return fused_shards(bands, mems, ensemble, *rest)
        return shards(ensemble, *rest)

    return jax.shard_map(
        body,
        mesh=mesh,
        in_specs=(
            P("mem", None, "band", None),
            P(("band", "mem"), None),
            P(("band", "mem"), None),
            P(("band", "mem")),
            P(("band", "mem"), None),
            P(("band", "mem"), None),
            P(("band", "mem"), None),
        ),
        out_specs=P("mem", None, "band", None),
        check_vma=False,
    )
```

```python
import functools

import jax
import jax.numpy as jnp
from jax import lax
from jax.experimental import pallas as pl
from jax.experimental.pallas import tpu as pltpu
from jax.sharding import PartitionSpec as P

TILE = 16
NSI = 6
STEPS = 2


COURANT = 0.08
HIGHEST = lax.Precision.HIGHEST
MESH = pl.DeviceIdType.MESH
CUTS = 2


def extended_2(block, sides, width):
    for axis, dim in sides:
        count = lax.axis_size(axis)
        forward = [(i, i + 1) for i in range(count - 1)]
        backward = [(target, source) for source, target in forward]
        low = lax.ppermute(
            lax.slice_in_dim(block, block.shape[dim] - width, None, axis=dim), axis, forward
        )
        high = lax.ppermute(lax.slice_in_dim(block, 0, width, axis=dim), axis, backward)
        block = jnp.concatenate([low, block, high], axis=dim)
    return block


def minmod(lower_jump, upper_jump):
    return jnp.maximum(0.0, jnp.minimum(lower_jump, upper_jump)) + jnp.minimum(
        0.0, jnp.maximum(lower_jump, upper_jump)
    )


def flux_divergence(halo_extended_field, sweep_direction, advected_field):
    extent = halo_extended_field.shape[sweep_direction]
    differences = lax.slice_in_dim(
        halo_extended_field, 1, extent, axis=sweep_direction
    ) - lax.slice_in_dim(halo_extended_field, 0, extent - 1, axis=sweep_direction)
    slopes = minmod(
        lax.slice_in_dim(differences, 0, extent - 2, axis=sweep_direction),
        lax.slice_in_dim(differences, 1, extent - 1, axis=sweep_direction),
    )
    state_left_side = lax.slice_in_dim(
        halo_extended_field, 1, extent - 2, axis=sweep_direction
    ) + 0.5 * lax.slice_in_dim(slopes, 0, extent - 3, axis=sweep_direction)
    state_right_side = lax.slice_in_dim(
        halo_extended_field, 2, extent - 1, axis=sweep_direction
    ) - 0.5 * lax.slice_in_dim(slopes, 1, extent - 2, axis=sweep_direction)
    advected_field_left = state_left_side[:, advected_field : advected_field + 1]
    advected_field_right = state_right_side[:, advected_field : advected_field + 1]
    signal_velocity = jnp.maximum(jnp.abs(advected_field_left), jnp.abs(advected_field_right))
    interface_fluxes = 0.5 * (
        advected_field_left * state_left_side + advected_field_right * state_right_side
    ) - 0.5 * signal_velocity * (state_right_side - state_left_side)
    return lax.slice_in_dim(
        interface_fluxes, 1, extent - 3, axis=sweep_direction
    ) - lax.slice_in_dim(interface_fluxes, 0, extent - 4, axis=sweep_direction)


def advance(halo_extended_field):
    centre = halo_extended_field[:, :, 2:-2]
    lat_div = flux_divergence(halo_extended_field, 2, 1)
    wrapped = jnp.concatenate([centre[..., -2:], centre, centre[..., :2]], axis=3)
    lon_div = flux_divergence(wrapped, 3, 0)
    return centre - COURANT * (lat_div + lon_div)


def obs_space(tile_state, obs_value, obs_site):
    site_count = tile_state.shape[2]
    ens_mean = jnp.mean(tile_state, axis=1)
    anomaly = tile_state - ens_mean[:, None, :]
    selector = (obs_site[:, :, None] == jnp.arange(site_count)[None, None, :]).astype(jnp.float32)
    obs_anomaly = jnp.einsum("bos,bks->bok", selector, anomaly, precision=HIGHEST)
    obs_mean = jnp.einsum("bos,bs->bo", selector, ens_mean, precision=HIGHEST)
    return (ens_mean, anomaly, obs_anomaly, obs_value - obs_mean)


def transform(local_anomaly, local_innovation, local_weight, ens_mean, anomaly):
    members = local_anomaly.shape[2]
    identity = jnp.eye(members, dtype=jnp.float32)
    weighted = local_anomaly * local_weight[:, :, None]
    gram_matrix = (
        jnp.einsum("bpk,bpj->bkj", weighted, local_anomaly, precision=HIGHEST)
        + (members - 1.0) * identity
    )
    frob_norm = jnp.sqrt(jnp.sum(gram_matrix * gram_matrix, axis=(1, 2)))
    root_iter = gram_matrix / frob_norm[:, None, None]
    inverse = jnp.broadcast_to(identity, gram_matrix.shape)
    for sweep in range(NSI):
        factor = 1.5 * identity - 0.5 * jnp.matmul(inverse, root_iter, precision=HIGHEST)
        root_iter = jnp.matmul(root_iter, factor, precision=HIGHEST)
        inverse = jnp.matmul(factor, inverse, precision=HIGHEST)
    projected = jnp.einsum("bpk,bp->bk", weighted, local_innovation, precision=HIGHEST)
    halfway = jnp.einsum("bkj,bj->bk", inverse, projected, precision=HIGHEST)
    mean_weights = (
        jnp.einsum("bkj,bj->bk", inverse, halfway, precision=HIGHEST) / frob_norm[:, None]
    )
    spread_weights = inverse * jnp.sqrt((members - 1.0) / frob_norm)[:, None, None]
    combined = spread_weights + mean_weights[:, :, None]
    return ens_mean[:, None, :] + jnp.einsum("bjk,bjs->bks", combined, anomaly, precision=HIGHEST)


def localise(obs_anomaly, innovation, slot_weight, neighbour_tiles, loc_weight, ens_mean, anomaly):
    batch_tiles = neighbour_tiles.shape[0]
    local_anomaly = obs_anomaly[neighbour_tiles].reshape(batch_tiles, -1, obs_anomaly.shape[2])
    local_innovation = innovation[neighbour_tiles].reshape(batch_tiles, -1)
    local_weight = (loc_weight[:, :, None] * slot_weight[neighbour_tiles]).reshape(batch_tiles, -1)
    return transform(local_anomaly, local_innovation, local_weight, ens_mean, anomaly)


def shards(ensemble, obs_value, obs_site, obs_count, obs_precision, loc_weight, neighbours):
    fields = ensemble
    lat_rows = fields.shape[2]
    margin = 2 * STEPS
    extended = extended_2(fields, (("band", 2),), margin)
    offset = lax.axis_index("band") * lat_rows
    lat_total = lat_rows * lax.axis_size("band")
    for repeat in range(STEPS):
        extended = advance(extended)
        remaining = margin - 2 * (repeat + 1)
        if remaining > 0:
            global_row = (
                lax.broadcasted_iota(jnp.int32, (1, 1, extended.shape[2], 1), 2)
                - remaining
                + offset
            )
            inside = (global_row >= 0) & (global_row < lat_total)
            extended = jnp.where(inside, extended, 0.0)
    fields = extended
    members, variables, lon_total = (fields.shape[0], fields.shape[1], fields.shape[3])
    flattened = fields.reshape(members, variables, lat_rows * lon_total)
    grouped = lax.all_to_all(flattened, "mem", split_axis=2, concat_axis=0, tiled=True)
    all_members = grouped.shape[0]
    tile_count = neighbours.shape[0]
    tile_state = (
        grouped.reshape(all_members, variables, tile_count, TILE)
        .transpose(2, 0, 1, 3)
        .reshape(tile_count, all_members, variables * TILE)
    )
    ens_mean, anomaly, obs_anomaly, innovation = obs_space(tile_state, obs_value, obs_site)
    live_slots = jnp.arange(obs_value.shape[1])[None, :] < obs_count[:, None]
    slot_weight = jnp.where(live_slots, obs_precision, 0.0)
    analysed = localise(
        obs_anomaly, innovation, slot_weight, neighbours, loc_weight, ens_mean, anomaly
    )
    outgoing = (
        analysed.reshape(tile_count, all_members, variables, TILE)
        .transpose(1, 2, 0, 3)
        .reshape(all_members, variables, tile_count * TILE)
    )
    returned = lax.all_to_all(outgoing, "mem", split_axis=0, concat_axis=2, tiled=True)
    fields = returned.reshape(members, variables, lat_rows, lon_total)
    return advance(extended_2(fields, (("band", 2),), 2))


def split_pair(x):
    high = x.astype(jnp.bfloat16)
    low = (x - high.astype(jnp.float32)).astype(jnp.bfloat16)
    return high, low


def left_form(x):
    return jnp.concatenate(split_pair(x), axis=1)


def right_form(x):
    wide = jnp.concatenate(split_pair(x), axis=1)
    return jnp.concatenate([wide, wide], axis=0)


def pair_dot(left, right):
    both = jnp.dot(left, right, preferred_element_type=jnp.float32)
    half = both.shape[1] // 2
    return both[:, :half] + both[:, half:]


def upwind(left, right, carrier):
    a_left = left[carrier : carrier + 1]
    a_right = right[carrier : carrier + 1]
    speed = jnp.maximum(jnp.abs(a_left), jnp.abs(a_right))
    return 0.5 * (a_left * left + a_right * right) - 0.5 * speed * (right - left)


def lon_divergence(row):
    size = row.shape[2]
    jump = pltpu.roll(row, size - 1, 2) - row
    half = 0.5 * minmod(pltpu.roll(jump, 1, 2), jump)
    flux = upwind(row + half, pltpu.roll(row - half, size - 1, 2), 0)
    return flux - pltpu.roll(flux, 1, 2)


def advance_rows(load, store, count, apart=False):
    rows = [load(i) for i in range(4)]
    jumps = [rows[i + 1] - rows[i] for i in range(3)]
    halves = [0.5 * minmod(jumps[i], jumps[i + 1]) for i in range(2)]
    lower = upwind(rows[1] + halves[0], rows[2] - halves[1], 1)
    for k in range(count):
        ahead = load(k + 4)
        jump = ahead - rows[3]
        half = 0.5 * minmod(jumps[2], jump)
        upper = upwind(rows[2] + halves[1], rows[3] - half, 1)
        centre = rows[2]
        change = (upper - lower) + lon_divergence(centre)
        if apart:
            store(k, centre, change)
        else:
            store(k, centre - COURANT * change)
        rows = rows[1:] + [ahead]
        jumps = jumps[1:] + [jump]
        halves = [halves[1], half]
        lower = upper


def cycle_kernel(
    bands,
    mems,
    loc_ref,
    near_ref,
    count_ref,
    x_ref,
    value_ref,
    site_ref,
    precision_ref,
    centre_ref,
    change_ref,
    first,
    second,
    third,
    state,
    weight_buf,
    target_buf,
    anomaly,
    means,
    gram,
    pull,
    root,
    inverse,
    turned,
    result,
    final,
    send_a,
    recv_a,
    send_b,
    recv_b,
    send_d,
    recv_d,
    local_sem,
):
    band = lax.axis_index("band")
    mem = lax.axis_index("mem")
    side = lax.rem(band, 2)
    base = band - side
    lon = x_ref.shape[1]
    half = state.shape[2]
    group = 2 * half
    nv = state.shape[1]
    lat = x_ref.shape[0] // (group * nv)
    span = nv * lat
    tiles = lon // TILE
    members = group * mems
    sites = nv * TILE
    me = side * mems + mem

    def greet(b, m, okay):
        @pl.when(okay)
        def _():
            pl.semaphore_signal(
                barrier, inc=1, device_id={"band": b, "mem": m}, device_id_type=MESH
            )

        return okay.astype(jnp.int32) if hasattr(okay, "astype") else jnp.int32(okay)

    barrier = pltpu.get_barrier_semaphore()
    partners = jnp.int32(0)
    for k in range(2 * mems):
        partners += greet(base + k // mems, jnp.int32(k % mems), me != k)
    near_band = jnp.where(side == 0, base - 1, base + 2)
    near_okay = (near_band >= 0) & (near_band < bands)
    for m in range(mems):
        partners += greet(near_band, jnp.int32(m), near_okay)
    past_band = jnp.where(side == 0, base - 2, base + 3)
    partners += greet(past_band, mem, near_okay)
    other_band = jnp.where(side == 0, base + 2, base - 1)
    other_okay = (other_band >= 0) & (other_band < bands)
    partners += greet(other_band, mem, other_okay)
    slots = value_ref.shape[1]
    slot_index = lax.broadcasted_iota(jnp.int32, (1, slots), 1)
    site_index = lax.broadcasted_iota(jnp.int32, (sites, slots), 0)
    for u in range(tiles):
        match = site_index == site_ref[u : u + 1, :]
        live = slot_index < count_ref[0, u]
        precision = jnp.where(live, precision_ref[u : u + 1, :], 0.0)
        weighted_value = precision * value_ref[u : u + 1, :]
        total = jnp.sum(jnp.where(match, precision, 0.0), axis=1, keepdims=True)
        weight_buf[u] = jnp.broadcast_to(total, (sites, members))
        total = jnp.sum(jnp.where(match, weighted_value, 0.0), axis=1, keepdims=True)
        target_buf[u] = jnp.broadcast_to(total, (sites, members))

    pl.semaphore_wait(barrier, partners)

    chunks = 4
    depth = half * span // chunks

    def copy_a(src, place, c, sem, target):
        return pltpu.make_async_remote_copy(
            src_ref=src,
            dst_ref=first.at[place, pl.ds(c * depth, depth), :],
            send_sem=send_a.at[sem, c],
            recv_sem=recv_a.at[place, c],
            device_id={"band": target, "mem": mem},
            device_id_type=MESH,
        )

    def own_part(h, c):
        return x_ref.at[pl.ds(h * half * span + c * depth, depth), :]

    own_a = pltpu.make_async_copy(
        x_ref.at[pl.ds(side * half * span, half * span), :], first.at[1 + side], local_sem.at[0]
    )
    partner = base + 1 - side
    got = 2 - side
    to_pair = [copy_a(own_part(1 - side, c), 1 + side, c, 0, partner) for c in range(chunks)]
    to_past = [copy_a(own_part(side, c), 3 - 3 * side, c, 1, past_band) for c in range(chunks)]
    relayed = [
        copy_a(first.at[got, pl.ds(c * depth, depth), :], 3 * side, c, 2, other_band)
        for c in range(chunks)
    ]

    for copy in to_pair:
        copy.start()

    @pl.when(near_okay)
    def _():
        for copy in to_past:
            copy.start()

    own_a.start()

    zeros = jnp.zeros((half * span, lon), jnp.float32)

    @pl.when(base == 0)
    def _():
        first[0] = zeros

    @pl.when(base == bands - 2)
    def _():
        first[3] = zeros

    def arrive(place, c):
        copy_a(own_part(side, c), place, c, 0, partner).wait_recv()

    for c in range(chunks):
        arrive(got, c)

        @pl.when(other_okay)
        def _():
            relayed[c].start()

    own_a.wait()
    edge = 2
    low_mask = jnp.where(base > 0, 1.0, 0.0)
    high_mask = jnp.where(base < bands - 2, 1.0, 0.0)
    block = 8
    parts = half // block

    def copy_b(part, k, sender):
        some = pl.ds(part * block, block)
        return pltpu.make_async_remote_copy(
            src_ref=third.at[k, :, some, :],
            dst_ref=state.at[sender, :, some, :],
            send_sem=send_b.at[part, k],
            recv_sem=recv_b.at[part, sender],
            device_id={"band": base + k // mems, "mem": jnp.int32(k % mems)},
            device_id_type=MESH,
        )

    def forecast_part(part):
        some = pl.ds(part * block, block)
        ready = range(part * chunks // parts, (part + 1) * chunks // parts)

        @pl.when(base > 0)
        def _():
            for c in ready:
                arrive(0, c)

        @pl.when(base < bands - 2)
        def _():
            for c in ready:
                arrive(3, c)

        def load_first(i):
            start = part * block * span + i % lat
            return jnp.stack(
                [first[i // lat, pl.ds(start + v * lat, block, stride=span), :] for v in range(nv)]
            )

        def store_second(k, row):
            if k < lat - edge:
                row = row * low_mask
            if k >= 3 * lat - edge:
                row = row * high_mask
            second[k, :, some, :] = row

        def store_third(k, row):
            third[k, :, some, :] = row

            @pl.when(me != k)
            def _():
                copy_b(part, k, me).start()

            @pl.when(me == k)
            def _():
                state[me, :, some, :] = row

        advance_rows(load_first, store_second, 4 * lat - 2 * edge)
        advance_rows(lambda i: second[i, :, some, :], store_third, 2 * lat)

    for part in range(parts):
        forecast_part(part)

    for part in range(parts):
        for k in range(2 * mems):

            @pl.when(me != k)
            def _():
                copy_b(part, k, jnp.int32(k)).wait_recv()

    for v in range(nv):
        pieces = [state[(k % 2) * mems + k // 2, v] for k in range(2 * mems)]
        field = jnp.concatenate(pieces, axis=0).T
        mean = jnp.mean(field, axis=1, keepdims=True)
        means[v] = jnp.broadcast_to(mean, (lon, members))
        anomaly[v] = field - mean

    def of_tile(ref, u):
        return jnp.concatenate([ref[v, u * TILE : (u + 1) * TILE, :] for v in range(nv)], axis=0)

    for u in range(tiles):
        p = of_tile(anomaly, u)
        d = weight_buf[u]
        p_high, p_low = split_pair(p)
        w_high, w_low = split_pair(p * d)
        gram[u] = lax.dot_general(
            jnp.concatenate([w_high, w_low, w_high], axis=0),
            jnp.concatenate([p_high, p_high, p_low], axis=0),
            (((0,), (0,)), ((), ())),
            preferred_element_type=jnp.float32,
        )
        pull[u] = jnp.sum(p * (target_buf[u] - d * of_tile(means, u)), axis=0, keepdims=True)

    identity = (
        lax.broadcasted_iota(jnp.int32, (members, members), 0)
        == lax.broadcasted_iota(jnp.int32, (members, members), 1)
    ).astype(jnp.float32)
    listed = near_ref.shape[0]
    norms = []
    drives = []
    for t in range(tiles):
        a = (members - 1.0) * identity
        drive = jnp.zeros((1, members), jnp.float32)
        for j in range(listed):
            u = near_ref[j, t]
            scale = loc_ref[j, t]
            a += scale * gram[u]
            drive += scale * pull[u]
        norm = jnp.sqrt(jnp.sum(jnp.sum(a * a, axis=1, keepdims=True), axis=0, keepdims=True))
        norms.append(norm)
        drives.append(drive)
        r = a * (1.0 / norm)
        s = 1.5 * identity - 0.5 * r
        root[t] = pair_dot(left_form(r), right_form(s))
        inverse[t] = s

    width = lon // CUTS
    packed = group // CUTS

    def copy_d(cut, m, place, sem, target):
        return pltpu.make_async_remote_copy(
            src_ref=result.at[cut, :, pl.ds(m * group, packed), :],
            dst_ref=final.at[place, cut],
            send_sem=send_d.at[cut, sem],
            recv_sem=recv_d.at[cut, place],
            device_id={"band": target, "mem": jnp.int32(m)},
            device_id_type=MESH,
        )

    outward = 1 - 2 * (mem < edge).astype(jnp.int32)
    out_band = band + outward
    out_okay = (out_band >= 0) & (out_band < bands)
    out_place = mem + edge - outward * lat

    def own_d(cut):
        return pltpu.make_async_copy(
            result.at[cut, :, pl.ds(mem * group, packed), :],
            final.at[mem + edge, cut],
            local_sem.at[1 + cut],
        )

    blank = jnp.zeros((edge, CUTS, nv, packed, lon), jnp.float32)

    @pl.when(band == 0)
    def _():
        final[0:edge] = blank

    @pl.when(band == bands - 1)
    def _():
        final[lat + edge : lat + 2 * edge] = blank

    def analyse_cut(cut):
        chosen = range(cut * tiles // CUTS, (cut + 1) * tiles // CUTS)

        def sweep(_, carry):
            for t in chosen:
                r, z = root[t], inverse[t]
                r_left, r_right = left_form(r), right_form(r)
                s = 1.5 * identity - 0.5 * pair_dot(left_form(z), r_right)
                root[t] = pair_dot(r_left, right_form(s))
                inverse[t] = pair_dot(left_form(s), right_form(z))
            return carry

        lax.fori_loop(0, NSI - 2, sweep, 0)

        for t in chosen:
            r, z = root[t], inverse[t]
            s = 1.5 * identity - 0.5 * pair_dot(left_form(z), right_form(r))
            z = pair_dot(left_form(s), right_form(z))
            p = of_tile(anomaly, t)
            stacked = jnp.concatenate([p, jnp.broadcast_to(drives[t], (TILE, members))], axis=0)
            applied = pair_dot(left_form(stacked), right_form(z))
            q = applied[:sites]
            step = applied[sites : sites + 1]
            shift = jnp.sum(q * step, axis=1, keepdims=True) / norms[t]
            new = of_tile(means, t) + q * jnp.sqrt((members - 1.0) / norms[t]) + shift
            for v in range(nv):
                turned[v, t * TILE : (t + 1) * TILE, :] = new[v * TILE : (v + 1) * TILE, :]

        for v in range(nv):
            cells = turned[v, cut * width : (cut + 1) * width, :]
            shifted = [cells] + [
                pltpu.roll(cells, members - k * packed, 1) for k in range(1, CUTS)
            ]
            result[cut, v] = jnp.concatenate(shifted, axis=0).T

        for m in range(mems):

            @pl.when(out_okay)
            def _():
                copy_d(cut, m, out_place, mems + m, out_band).start()

        for m in range(mems):

            @pl.when(mem != m)
            def _():
                copy_d(cut, m, mem + edge, m, band).start()

        own_d(cut).start()

    for cut in range(CUTS):
        analyse_cut(cut)

    for cut in range(CUTS):
        own_d(cut).wait()
        for k in range(lat + 2 * edge):
            if k < edge:
                okay = band > 0
            elif k < lat + edge:
                okay = mem != k - edge
            else:
                okay = band < bands - 1

            @pl.when(okay)
            def _():
                copy_d(cut, 0, k, 0, band).wait_recv()

    strip = lax.broadcasted_iota(jnp.int32, (1, 1, lon), 2) // width

    def load_final(i):
        cuts = [final[i, cut] for cut in range(CUTS)]
        pieces = []
        for k in range(CUTS):
            piece = None
            for cut in range(CUTS):
                placed = cuts[cut]
                if cut != k:
                    placed = pltpu.roll(placed, ((cut - k) * width) % lon, 2)
                piece = placed if piece is None else jnp.where(strip == cut, placed, piece)
            pieces.append(piece)
        return jnp.concatenate(pieces, axis=1)

    def store_out(k, centre, change):
        for v in range(nv):
            spots = pl.ds(v * lat + k, group, stride=span)
            centre_ref[spots, :] = centre[v]
            change_ref[spots, :] = change[v]

    advance_rows(load_final, store_out, lat, apart=True)

    for copy in to_pair:
        copy.wait_send()

    @pl.when(near_okay)
    def _():
        for copy in to_past:
            copy.wait_send()

    @pl.when(other_okay)
    def _():
        for copy in relayed:
            copy.wait_send()

    for part in range(parts):
        for k in range(2 * mems):

            @pl.when(me != k)
            def _():
                copy_b(part, k, me).wait_send()

    for cut in range(CUTS):
        for m in range(mems):

            @pl.when(out_okay)
            def _():
                copy_d(cut, m, out_place, mems + m, out_band).wait_send()

            @pl.when(mem != m)
            def _():
                copy_d(cut, m, mem + edge, m, band).wait_send()


def fused_shards(
    bands, mems, ensemble, obs_value, obs_site, obs_count, obs_precision, loc_weight, neighbours
):
    group, nv, lat, lon = ensemble.shape
    half = group // 2
    tiles = lon // TILE
    members = group * mems
    sites = nv * TILE
    edge = 2
    f32 = jnp.float32
    vmem = pl.BlockSpec(memory_space=pltpu.VMEM)
    smem = pl.BlockSpec(memory_space=pltpu.SMEM)
    centre, change = pl.pallas_call(
        functools.partial(cycle_kernel, bands, mems),
        out_shape=[jax.ShapeDtypeStruct((group * nv * lat, lon), f32)] * 2,
        in_specs=[smem] * 3 + [pl.BlockSpec(memory_space=pl.ANY)] + [vmem] * 3,
        out_specs=[vmem] * 2,
        scratch_shapes=[
            pltpu.VMEM((4, half * nv * lat, lon), f32),
            pltpu.VMEM((4 * lat - 2 * edge, nv, half, lon), f32),
            pltpu.VMEM((2 * lat, nv, half, lon), f32),
            pltpu.VMEM((2 * mems, nv, half, lon), f32),
            pltpu.VMEM((tiles, sites, members), f32),
            pltpu.VMEM((tiles, sites, members), f32),
            pltpu.VMEM((nv, lon, members), f32),
            pltpu.VMEM((nv, lon, members), f32),
            pltpu.VMEM((tiles, members, members), f32),
            pltpu.VMEM((tiles, 1, members), f32),
            pltpu.VMEM((tiles, members, members), f32),
            pltpu.VMEM((tiles, members, members), f32),
            pltpu.VMEM((nv, lon, members), f32),
            pltpu.VMEM((CUTS, nv, members, lon), f32),
            pltpu.VMEM((lat + 2 * edge, CUTS, nv, group // CUTS, lon), f32),
            pltpu.SemaphoreType.DMA((3, 4)),
            pltpu.SemaphoreType.DMA((4, 4)),
            pltpu.SemaphoreType.DMA((half // 8, 2 * mems)),
            pltpu.SemaphoreType.DMA((half // 8, 2 * mems)),
            pltpu.SemaphoreType.DMA((CUTS, 2 * mems)),
            pltpu.SemaphoreType.DMA((CUTS, lat + 2 * edge)),
            pltpu.SemaphoreType.DMA((1 + CUTS,)),
        ],
        compiler_params=pltpu.CompilerParams(collective_id=0, has_side_effects=True),
    )(
        loc_weight.T,
        neighbours.T,
        obs_count[None, :],
        ensemble.reshape(group * nv * lat, lon),
        obs_value,
        obs_site,
        obs_precision,
    )
    return (centre - COURANT * change).reshape(ensemble.shape)


def solution(mesh):
    bands, mems = mesh.shape["band"], mesh.shape["mem"]

    def body(ensemble, *rest):
        group, _, lat, lon = ensemble.shape
        fits = (
            STEPS == 2
            and lat == 4
            and lat == mems
            and bands % 2 == 0
            and group % 16 == 0
            and lon == group * mems == 128
        )
        if fits:
            return fused_shards(bands, mems, ensemble, *rest)
        return shards(ensemble, *rest)

    return jax.shard_map(
        body,
        mesh=mesh,
        in_specs=(
            P("mem", None, "band", None),
            P(("band", "mem"), None),
            P(("band", "mem"), None),
            P(("band", "mem")),
            P(("band", "mem"), None),
            P(("band", "mem"), None),
            P(("band", "mem"), None),
        ),
        out_specs=P("mem", None, "band", None),
        check_vma=False,
    )
```

```python
import functools

import jax
import jax.numpy as jnp
from jax import lax
from jax.experimental import pallas as pl
from jax.experimental.pallas import tpu as pltpu
from jax.sharding import PartitionSpec as P

TILE = 16
NSI = 6
STEPS = 2


COURANT = 0.08
HIGHEST = lax.Precision.HIGHEST
MESH = pl.DeviceIdType.MESH
CUTS = 2


def extended_2(block, sides, width):
    for axis, dim in sides:
        count = lax.axis_size(axis)
        forward = [(i, i + 1) for i in range(count - 1)]
        backward = [(target, source) for source, target in forward]
        low = lax.ppermute(
            lax.slice_in_dim(block, block.shape[dim] - width, None, axis=dim), axis, forward
        )
        high = lax.ppermute(lax.slice_in_dim(block, 0, width, axis=dim), axis, backward)
        block = jnp.concatenate([low, block, high], axis=dim)
    return block


def minmod(lower_jump, upper_jump):
    return jnp.maximum(0.0, jnp.minimum(lower_jump, upper_jump)) + jnp.minimum(
        0.0, jnp.maximum(lower_jump, upper_jump)
    )


def flux_divergence(halo_extended_field, sweep_direction, advected_field):
    extent = halo_extended_field.shape[sweep_direction]
    differences = lax.slice_in_dim(
        halo_extended_field, 1, extent, axis=sweep_direction
    ) - lax.slice_in_dim(halo_extended_field, 0, extent - 1, axis=sweep_direction)
    slopes = minmod(
        lax.slice_in_dim(differences, 0, extent - 2, axis=sweep_direction),
        lax.slice_in_dim(differences, 1, extent - 1, axis=sweep_direction),
    )
    state_left_side = lax.slice_in_dim(
        halo_extended_field, 1, extent - 2, axis=sweep_direction
    ) + 0.5 * lax.slice_in_dim(slopes, 0, extent - 3, axis=sweep_direction)
    state_right_side = lax.slice_in_dim(
        halo_extended_field, 2, extent - 1, axis=sweep_direction
    ) - 0.5 * lax.slice_in_dim(slopes, 1, extent - 2, axis=sweep_direction)
    advected_field_left = state_left_side[:, advected_field : advected_field + 1]
    advected_field_right = state_right_side[:, advected_field : advected_field + 1]
    signal_velocity = jnp.maximum(jnp.abs(advected_field_left), jnp.abs(advected_field_right))
    interface_fluxes = 0.5 * (
        advected_field_left * state_left_side + advected_field_right * state_right_side
    ) - 0.5 * signal_velocity * (state_right_side - state_left_side)
    return lax.slice_in_dim(
        interface_fluxes, 1, extent - 3, axis=sweep_direction
    ) - lax.slice_in_dim(interface_fluxes, 0, extent - 4, axis=sweep_direction)


def advance(halo_extended_field):
    centre = halo_extended_field[:, :, 2:-2]
    lat_div = flux_divergence(halo_extended_field, 2, 1)
    wrapped = jnp.concatenate([centre[..., -2:], centre, centre[..., :2]], axis=3)
    lon_div = flux_divergence(wrapped, 3, 0)
    return centre - COURANT * (lat_div + lon_div)


def obs_space(tile_state, obs_value, obs_site):
    site_count = tile_state.shape[2]
    ens_mean = jnp.mean(tile_state, axis=1)
    anomaly = tile_state - ens_mean[:, None, :]
    selector = (obs_site[:, :, None] == jnp.arange(site_count)[None, None, :]).astype(jnp.float32)
    obs_anomaly = jnp.einsum("bos,bks->bok", selector, anomaly, precision=HIGHEST)
    obs_mean = jnp.einsum("bos,bs->bo", selector, ens_mean, precision=HIGHEST)
    return (ens_mean, anomaly, obs_anomaly, obs_value - obs_mean)


def transform(local_anomaly, local_innovation, local_weight, ens_mean, anomaly):
    members = local_anomaly.shape[2]
    identity = jnp.eye(members, dtype=jnp.float32)
    weighted = local_anomaly * local_weight[:, :, None]
    gram_matrix = (
        jnp.einsum("bpk,bpj->bkj", weighted, local_anomaly, precision=HIGHEST)
        + (members - 1.0) * identity
    )
    frob_norm = jnp.sqrt(jnp.sum(gram_matrix * gram_matrix, axis=(1, 2)))
    root_iter = gram_matrix / frob_norm[:, None, None]
    inverse = jnp.broadcast_to(identity, gram_matrix.shape)
    for sweep in range(NSI):
        factor = 1.5 * identity - 0.5 * jnp.matmul(inverse, root_iter, precision=HIGHEST)
        root_iter = jnp.matmul(root_iter, factor, precision=HIGHEST)
        inverse = jnp.matmul(factor, inverse, precision=HIGHEST)
    projected = jnp.einsum("bpk,bp->bk", weighted, local_innovation, precision=HIGHEST)
    halfway = jnp.einsum("bkj,bj->bk", inverse, projected, precision=HIGHEST)
    mean_weights = (
        jnp.einsum("bkj,bj->bk", inverse, halfway, precision=HIGHEST) / frob_norm[:, None]
    )
    spread_weights = inverse * jnp.sqrt((members - 1.0) / frob_norm)[:, None, None]
    combined = spread_weights + mean_weights[:, :, None]
    return ens_mean[:, None, :] + jnp.einsum("bjk,bjs->bks", combined, anomaly, precision=HIGHEST)


def localise(obs_anomaly, innovation, slot_weight, neighbour_tiles, loc_weight, ens_mean, anomaly):
    batch_tiles = neighbour_tiles.shape[0]
    local_anomaly = obs_anomaly[neighbour_tiles].reshape(batch_tiles, -1, obs_anomaly.shape[2])
    local_innovation = innovation[neighbour_tiles].reshape(batch_tiles, -1)
    local_weight = (loc_weight[:, :, None] * slot_weight[neighbour_tiles]).reshape(batch_tiles, -1)
    return transform(local_anomaly, local_innovation, local_weight, ens_mean, anomaly)


def shards(ensemble, obs_value, obs_site, obs_count, obs_precision, loc_weight, neighbours):
    fields = ensemble
    lat_rows = fields.shape[2]
    margin = 2 * STEPS
    extended = extended_2(fields, (("band", 2),), margin)
    offset = lax.axis_index("band") * lat_rows
    lat_total = lat_rows * lax.axis_size("band")
    for repeat in range(STEPS):
        extended = advance(extended)
        remaining = margin - 2 * (repeat + 1)
        if remaining > 0:
            global_row = (
                lax.broadcasted_iota(jnp.int32, (1, 1, extended.shape[2], 1), 2)
                - remaining
                + offset
            )
            inside = (global_row >= 0) & (global_row < lat_total)
            extended = jnp.where(inside, extended, 0.0)
    fields = extended
    members, variables, lon_total = (fields.shape[0], fields.shape[1], fields.shape[3])
    flattened = fields.reshape(members, variables, lat_rows * lon_total)
    grouped = lax.all_to_all(flattened, "mem", split_axis=2, concat_axis=0, tiled=True)
    all_members = grouped.shape[0]
    tile_count = neighbours.shape[0]
    tile_state = (
        grouped.reshape(all_members, variables, tile_count, TILE)
        .transpose(2, 0, 1, 3)
        .reshape(tile_count, all_members, variables * TILE)
    )
    ens_mean, anomaly, obs_anomaly, innovation = obs_space(tile_state, obs_value, obs_site)
    live_slots = jnp.arange(obs_value.shape[1])[None, :] < obs_count[:, None]
    slot_weight = jnp.where(live_slots, obs_precision, 0.0)
    analysed = localise(
        obs_anomaly, innovation, slot_weight, neighbours, loc_weight, ens_mean, anomaly
    )
    outgoing = (
        analysed.reshape(tile_count, all_members, variables, TILE)
        .transpose(1, 2, 0, 3)
        .reshape(all_members, variables, tile_count * TILE)
    )
    returned = lax.all_to_all(outgoing, "mem", split_axis=0, concat_axis=2, tiled=True)
    fields = returned.reshape(members, variables, lat_rows, lon_total)
    return advance(extended_2(fields, (("band", 2),), 2))


def split_pair(x):
    high = x.astype(jnp.bfloat16)
    low = (x - high.astype(jnp.float32)).astype(jnp.bfloat16)
    return high, low


def left_form(x):
    return jnp.concatenate(split_pair(x), axis=1)


def right_form(x):
    wide = jnp.concatenate(split_pair(x), axis=1)
    return jnp.concatenate([wide, wide], axis=0)


def pair_dot(left, right):
    both = jnp.dot(left, right, preferred_element_type=jnp.float32)
    half = both.shape[1] // 2
    return both[:, :half] + both[:, half:]


def upwind(left, right, carrier):
    a_left = left[carrier : carrier + 1]
    a_right = right[carrier : carrier + 1]
    speed = jnp.maximum(jnp.abs(a_left), jnp.abs(a_right))
    return 0.5 * (a_left * left + a_right * right) - 0.5 * speed * (right - left)


def lon_divergence(row):
    size = row.shape[2]
    jump = pltpu.roll(row, size - 1, 2) - row
    half = 0.5 * minmod(pltpu.roll(jump, 1, 2), jump)
    flux = upwind(row + half, pltpu.roll(row - half, size - 1, 2), 0)
    return flux - pltpu.roll(flux, 1, 2)


def advance_rows(load, store, count, apart=False):
    rows = [load(i) for i in range(4)]
    jumps = [rows[i + 1] - rows[i] for i in range(3)]
    halves = [0.5 * minmod(jumps[i], jumps[i + 1]) for i in range(2)]
    lower = upwind(rows[1] + halves[0], rows[2] - halves[1], 1)
    for k in range(count):
        ahead = load(k + 4)
        jump = ahead - rows[3]
        half = 0.5 * minmod(jumps[2], jump)
        upper = upwind(rows[2] + halves[1], rows[3] - half, 1)
        centre = rows[2]
        change = (upper - lower) + lon_divergence(centre)
        if apart:
            store(k, centre, change)
        else:
            store(k, centre - COURANT * change)
        rows = rows[1:] + [ahead]
        jumps = jumps[1:] + [jump]
        halves = [halves[1], half]
        lower = upper


def cycle_kernel(
    bands,
    mems,
    loc_ref,
    near_ref,
    count_ref,
    x_ref,
    value_ref,
    site_ref,
    precision_ref,
    centre_ref,
    change_ref,
    first,
    second,
    third,
    state,
    weight_buf,
    target_buf,
    anomaly,
    means,
    gram,
    pull,
    root,
    inverse,
    turned,
    result,
    final,
    send_a,
    recv_a,
    send_b,
    recv_b,
    send_d,
    recv_d,
    local_sem,
):
    band = lax.axis_index("band")
    mem = lax.axis_index("mem")
    side = lax.rem(band, 2)
    base = band - side
    lon = x_ref.shape[1]
    half = state.shape[2]
    group = 2 * half
    nv = state.shape[1]
    lat = x_ref.shape[0] // (group * nv)
    span = nv * lat
    tiles = lon // TILE
    members = group * mems
    sites = nv * TILE
    me = side * mems + mem

    def greet(b, m, okay):
        @pl.when(okay)
        def _():
            pl.semaphore_signal(
                barrier, inc=1, device_id={"band": b, "mem": m}, device_id_type=MESH
            )

        return okay.astype(jnp.int32) if hasattr(okay, "astype") else jnp.int32(okay)

    barrier = pltpu.get_barrier_semaphore()
    partners = jnp.int32(0)
    for k in range(2 * mems):
        partners += greet(base + k // mems, jnp.int32(k % mems), me != k)
    near_band = jnp.where(side == 0, base - 1, base + 2)
    near_okay = (near_band >= 0) & (near_band < bands)
    for m in range(mems):
        partners += greet(near_band, jnp.int32(m), near_okay)
    past_band = jnp.where(side == 0, base - 2, base + 3)
    partners += greet(past_band, mem, near_okay)
    other_band = jnp.where(side == 0, base + 2, base - 1)
    other_okay = (other_band >= 0) & (other_band < bands)
    partners += greet(other_band, mem, other_okay)
    slots = value_ref.shape[1]
    slot_index = lax.broadcasted_iota(jnp.int32, (1, slots), 1)
    site_index = lax.broadcasted_iota(jnp.int32, (sites, slots), 0)
    for u in range(tiles):
        match = site_index == site_ref[u : u + 1, :]
        live = slot_index < count_ref[0, u]
        precision = jnp.where(live, precision_ref[u : u + 1, :], 0.0)
        weighted_value = precision * value_ref[u : u + 1, :]
        total = jnp.sum(jnp.where(match, precision, 0.0), axis=1, keepdims=True)
        weight_buf[u] = jnp.broadcast_to(total, (sites, members))
        total = jnp.sum(jnp.where(match, weighted_value, 0.0), axis=1, keepdims=True)
        target_buf[u] = jnp.broadcast_to(total, (sites, members))

    pl.semaphore_wait(barrier, partners)

    chunks = 4
    depth = half * span // chunks

    def copy_a(src, place, c, sem, target):
        return pltpu.make_async_remote_copy(
            src_ref=src,
            dst_ref=first.at[place, pl.ds(c * depth, depth), :],
            send_sem=send_a.at[sem, c],
            recv_sem=recv_a.at[place, c],
            device_id={"band": target, "mem": mem},
            device_id_type=MESH,
        )

    def own_part(h, c):
        return x_ref.at[pl.ds(h * half * span + c * depth, depth), :]

    own_a = pltpu.make_async_copy(
        x_ref.at[pl.ds(side * half * span, half * span), :], first.at[1 + side], local_sem.at[0]
    )
    partner = base + 1 - side
    got = 2 - side
    to_pair = [copy_a(own_part(1 - side, c), 1 + side, c, 0, partner) for c in range(chunks)]
    to_past = [copy_a(own_part(side, c), 3 - 3 * side, c, 1, past_band) for c in range(chunks)]
    relayed = [
        copy_a(first.at[got, pl.ds(c * depth, depth), :], 3 * side, c, 2, other_band)
        for c in range(chunks)
    ]

    for copy in to_pair:
        copy.start()

    @pl.when(near_okay)
    def _():
        for copy in to_past:
            copy.start()

    own_a.start()

    zeros = jnp.zeros((half * span, lon), jnp.float32)

    @pl.when(base == 0)
    def _():
        first[0] = zeros

    @pl.when(base == bands - 2)
    def _():
        first[3] = zeros

    def arrive(place, c):
        copy_a(own_part(side, c), place, c, 0, partner).wait_recv()

    for c in range(chunks):
        arrive(got, c)

        @pl.when(other_okay)
        def _():
            relayed[c].start()

    own_a.wait()
    edge = 2
    low_mask = jnp.where(base > 0, 1.0, 0.0)
    high_mask = jnp.where(base < bands - 2, 1.0, 0.0)
    block = 8
    parts = half // block

    def copy_b(part, k, sender):
        some = pl.ds(part * block, block)
        return pltpu.make_async_remote_copy(
            src_ref=third.at[k, :, some, :],
            dst_ref=state.at[sender, :, some, :],
            send_sem=send_b.at[part, k],
            recv_sem=recv_b.at[part, sender],
            device_id={"band": base + k // mems, "mem": jnp.int32(k % mems)},
            device_id_type=MESH,
        )

    def forecast_part(part):
        some = pl.ds(part * block, block)
        ready = range(part * chunks // parts, (part + 1) * chunks // parts)

        @pl.when(base > 0)
        def _():
            for c in ready:
                arrive(0, c)

        @pl.when(base < bands - 2)
        def _():
            for c in ready:
                arrive(3, c)

        def load_first(i):
            start = part * block * span + i % lat
            return jnp.stack(
                [first[i // lat, pl.ds(start + v * lat, block, stride=span), :] for v in range(nv)]
            )

        def store_second(k, row):
            if k < lat - edge:
                row = row * low_mask
            if k >= 3 * lat - edge:
                row = row * high_mask
            second[k, :, some, :] = row

        def store_third(k, row):
            third[k, :, some, :] = row

            @pl.when(me != k)
            def _():
                copy_b(part, k, me).start()

            @pl.when(me == k)
            def _():
                state[me, :, some, :] = row

        advance_rows(load_first, store_second, 4 * lat - 2 * edge)
        advance_rows(lambda i: second[i, :, some, :], store_third, 2 * lat)

    for part in range(parts):
        forecast_part(part)

    for part in range(parts):
        for k in range(2 * mems):

            @pl.when(me != k)
            def _():
                copy_b(part, k, jnp.int32(k)).wait_recv()

    for v in range(nv):
        pieces = [state[(k % 2) * mems + k // 2, v] for k in range(2 * mems)]
        field = jnp.concatenate(pieces, axis=0).T
        mean = jnp.mean(field, axis=1, keepdims=True)
        means[v] = jnp.broadcast_to(mean, (lon, members))
        anomaly[v] = field - mean

    def of_tile(ref, u):
        return jnp.concatenate([ref[v, u * TILE : (u + 1) * TILE, :] for v in range(nv)], axis=0)

    for u in range(tiles):
        p = of_tile(anomaly, u)
        d = weight_buf[u]
        p_high, p_low = split_pair(p)
        w_high, w_low = split_pair(p * d)
        gram[u] = lax.dot_general(
            jnp.concatenate([w_high, w_low, w_high], axis=0),
            jnp.concatenate([p_high, p_high, p_low], axis=0),
            (((0,), (0,)), ((), ())),
            preferred_element_type=jnp.float32,
        )
        pull[u] = jnp.sum(p * (target_buf[u] - d * of_tile(means, u)), axis=0, keepdims=True)

    identity = (
        lax.broadcasted_iota(jnp.int32, (members, members), 0)
        == lax.broadcasted_iota(jnp.int32, (members, members), 1)
    ).astype(jnp.float32)
    listed = near_ref.shape[0]
    norms = []
    drives = []
    for t in range(tiles):
        a = (members - 1.0) * identity
        drive = jnp.zeros((1, members), jnp.float32)
        for j in range(listed):
            u = near_ref[j, t]
            scale = loc_ref[j, t]
            a += scale * gram[u]
            drive += scale * pull[u]
        norm = jnp.sqrt(jnp.sum(jnp.sum(a * a, axis=1, keepdims=True), axis=0, keepdims=True))
        norms.append(norm)
        drives.append(drive)
        r = a * (1.0 / norm)
        s = 1.5 * identity - 0.5 * r
        root[t] = pair_dot(left_form(r), right_form(s))
        inverse[t] = s

    width = lon // CUTS
    packed = group // CUTS

    def copy_d(cut, m, place, sem, target):
        return pltpu.make_async_remote_copy(
            src_ref=result.at[cut, :, pl.ds(m * group, packed), :],
            dst_ref=final.at[place, cut],
            send_sem=send_d.at[cut, sem],
            recv_sem=recv_d.at[cut, place],
            device_id={"band": target, "mem": jnp.int32(m)},
            device_id_type=MESH,
        )

    outward = 1 - 2 * (mem < edge).astype(jnp.int32)
    out_band = band + outward
    out_okay = (out_band >= 0) & (out_band < bands)
    out_place = mem + edge - outward * lat

    def own_d(cut):
        return pltpu.make_async_copy(
            result.at[cut, :, pl.ds(mem * group, packed), :],
            final.at[mem + edge, cut],
            local_sem.at[1 + cut],
        )

    blank = jnp.zeros((edge, CUTS, nv, packed, lon), jnp.float32)

    @pl.when(band == 0)
    def _():
        final[0:edge] = blank

    @pl.when(band == bands - 1)
    def _():
        final[lat + edge : lat + 2 * edge] = blank

    def analyse_cut(cut):
        chosen = range(cut * tiles // CUTS, (cut + 1) * tiles // CUTS)

        def sweep(_, carry):
            for t in chosen:
                r, z = root[t], inverse[t]
                r_left, r_right = left_form(r), right_form(r)
                s = 1.5 * identity - 0.5 * pair_dot(left_form(z), r_right)
                root[t] = pair_dot(r_left, right_form(s))
                inverse[t] = pair_dot(left_form(s), right_form(z))
            return carry

        lax.fori_loop(0, NSI - 2, sweep, 0, unroll=True)

        for t in chosen:
            r, z = root[t], inverse[t]
            s = 1.5 * identity - 0.5 * pair_dot(left_form(z), right_form(r))
            z = pair_dot(left_form(s), right_form(z))
            p = of_tile(anomaly, t)
            stacked = jnp.concatenate([p, jnp.broadcast_to(drives[t], (TILE, members))], axis=0)
            applied = pair_dot(left_form(stacked), right_form(z))
            q = applied[:sites]
            step = applied[sites : sites + 1]
            shift = jnp.sum(q * step, axis=1, keepdims=True) / norms[t]
            new = of_tile(means, t) + q * jnp.sqrt((members - 1.0) / norms[t]) + shift
            for v in range(nv):
                turned[v, t * TILE : (t + 1) * TILE, :] = new[v * TILE : (v + 1) * TILE, :]

        for v in range(nv):
            cells = turned[v, cut * width : (cut + 1) * width, :]
            shifted = [cells] + [
                pltpu.roll(cells, members - k * packed, 1) for k in range(1, CUTS)
            ]
            result[cut, v] = jnp.concatenate(shifted, axis=0).T

        for m in range(mems):

            @pl.when(out_okay)
            def _():
                copy_d(cut, m, out_place, mems + m, out_band).start()

        for m in range(mems):

            @pl.when(mem != m)
            def _():
                copy_d(cut, m, mem + edge, m, band).start()

        own_d(cut).start()

    for cut in range(CUTS):
        analyse_cut(cut)

    for cut in range(CUTS):
        own_d(cut).wait()
        for k in range(lat + 2 * edge):
            if k < edge:
                okay = band > 0
            elif k < lat + edge:
                okay = mem != k - edge
            else:
                okay = band < bands - 1

            @pl.when(okay)
            def _():
                copy_d(cut, 0, k, 0, band).wait_recv()

    strip = lax.broadcasted_iota(jnp.int32, (1, 1, lon), 2) // width

    def load_final(i):
        cuts = [final[i, cut] for cut in range(CUTS)]
        pieces = []
        for k in range(CUTS):
            piece = None
            for cut in range(CUTS):
                placed = cuts[cut]
                if cut != k:
                    placed = pltpu.roll(placed, ((cut - k) * width) % lon, 2)
                piece = placed if piece is None else jnp.where(strip == cut, placed, piece)
            pieces.append(piece)
        return jnp.concatenate(pieces, axis=1)

    def store_out(k, centre, change):
        for v in range(nv):
            spots = pl.ds(v * lat + k, group, stride=span)
            centre_ref[spots, :] = centre[v]
            change_ref[spots, :] = change[v]

    advance_rows(load_final, store_out, lat, apart=True)

    for copy in to_pair:
        copy.wait_send()

    @pl.when(near_okay)
    def _():
        for copy in to_past:
            copy.wait_send()

    @pl.when(other_okay)
    def _():
        for copy in relayed:
            copy.wait_send()

    for part in range(parts):
        for k in range(2 * mems):

            @pl.when(me != k)
            def _():
                copy_b(part, k, me).wait_send()

    for cut in range(CUTS):
        for m in range(mems):

            @pl.when(out_okay)
            def _():
                copy_d(cut, m, out_place, mems + m, out_band).wait_send()

            @pl.when(mem != m)
            def _():
                copy_d(cut, m, mem + edge, m, band).wait_send()


def fused_shards(
    bands, mems, ensemble, obs_value, obs_site, obs_count, obs_precision, loc_weight, neighbours
):
    group, nv, lat, lon = ensemble.shape
    half = group // 2
    tiles = lon // TILE
    members = group * mems
    sites = nv * TILE
    edge = 2
    f32 = jnp.float32
    vmem = pl.BlockSpec(memory_space=pltpu.VMEM)
    smem = pl.BlockSpec(memory_space=pltpu.SMEM)
    centre, change = pl.pallas_call(
        functools.partial(cycle_kernel, bands, mems),
        out_shape=[jax.ShapeDtypeStruct((group * nv * lat, lon), f32)] * 2,
        in_specs=[smem] * 3 + [pl.BlockSpec(memory_space=pl.ANY)] + [vmem] * 3,
        out_specs=[vmem] * 2,
        scratch_shapes=[
            pltpu.VMEM((4, half * nv * lat, lon), f32),
            pltpu.VMEM((4 * lat - 2 * edge, nv, half, lon), f32),
            pltpu.VMEM((2 * lat, nv, half, lon), f32),
            pltpu.VMEM((2 * mems, nv, half, lon), f32),
            pltpu.VMEM((tiles, sites, members), f32),
            pltpu.VMEM((tiles, sites, members), f32),
            pltpu.VMEM((nv, lon, members), f32),
            pltpu.VMEM((nv, lon, members), f32),
            pltpu.VMEM((tiles, members, members), f32),
            pltpu.VMEM((tiles, 1, members), f32),
            pltpu.VMEM((tiles, members, members), f32),
            pltpu.VMEM((tiles, members, members), f32),
            pltpu.VMEM((nv, lon, members), f32),
            pltpu.VMEM((CUTS, nv, members, lon), f32),
            pltpu.VMEM((lat + 2 * edge, CUTS, nv, group // CUTS, lon), f32),
            pltpu.SemaphoreType.DMA((3, 4)),
            pltpu.SemaphoreType.DMA((4, 4)),
            pltpu.SemaphoreType.DMA((half // 8, 2 * mems)),
            pltpu.SemaphoreType.DMA((half // 8, 2 * mems)),
            pltpu.SemaphoreType.DMA((CUTS, 2 * mems)),
            pltpu.SemaphoreType.DMA((CUTS, lat + 2 * edge)),
            pltpu.SemaphoreType.DMA((1 + CUTS,)),
        ],
        compiler_params=pltpu.CompilerParams(collective_id=0, has_side_effects=True),
    )(
        loc_weight.T,
        neighbours.T,
        obs_count[None, :],
        ensemble.reshape(group * nv * lat, lon),
        obs_value,
        obs_site,
        obs_precision,
    )
    return (centre - COURANT * change).reshape(ensemble.shape)


def solution(mesh):
    bands, mems = mesh.shape["band"], mesh.shape["mem"]

    def body(ensemble, *rest):
        group, _, lat, lon = ensemble.shape
        fits = (
            STEPS == 2
            and lat == 4
            and lat == mems
            and bands % 2 == 0
            and group % 16 == 0
            and lon == group * mems == 128
        )
        if fits:
            return fused_shards(bands, mems, ensemble, *rest)
        return shards(ensemble, *rest)

    return jax.shard_map(
        body,
        mesh=mesh,
        in_specs=(
            P("mem", None, "band", None),
            P(("band", "mem"), None),
            P(("band", "mem"), None),
            P(("band", "mem")),
            P(("band", "mem"), None),
            P(("band", "mem"), None),
            P(("band", "mem"), None),
        ),
        out_specs=P("mem", None, "band", None),
        check_vma=False,
    )
```

```python
import functools

import jax
import jax.numpy as jnp
from jax import lax
from jax.experimental import pallas as pl
from jax.experimental.pallas import tpu as pltpu
from jax.sharding import PartitionSpec as P

TILE = 16
NSI = 6
STEPS = 2


COURANT = 0.08
HIGHEST = lax.Precision.HIGHEST
MESH = pl.DeviceIdType.MESH
CUTS = 2


def extended_2(block, sides, width):
    for axis, dim in sides:
        count = lax.axis_size(axis)
        forward = [(i, i + 1) for i in range(count - 1)]
        backward = [(target, source) for source, target in forward]
        low = lax.ppermute(
            lax.slice_in_dim(block, block.shape[dim] - width, None, axis=dim), axis, forward
        )
        high = lax.ppermute(lax.slice_in_dim(block, 0, width, axis=dim), axis, backward)
        block = jnp.concatenate([low, block, high], axis=dim)
    return block


def minmod(lower_jump, upper_jump):
    return jnp.maximum(0.0, jnp.minimum(lower_jump, upper_jump)) + jnp.minimum(
        0.0, jnp.maximum(lower_jump, upper_jump)
    )


def flux_divergence(halo_extended_field, sweep_direction, advected_field):
    extent = halo_extended_field.shape[sweep_direction]
    differences = lax.slice_in_dim(
        halo_extended_field, 1, extent, axis=sweep_direction
    ) - lax.slice_in_dim(halo_extended_field, 0, extent - 1, axis=sweep_direction)
    slopes = minmod(
        lax.slice_in_dim(differences, 0, extent - 2, axis=sweep_direction),
        lax.slice_in_dim(differences, 1, extent - 1, axis=sweep_direction),
    )
    state_left_side = lax.slice_in_dim(
        halo_extended_field, 1, extent - 2, axis=sweep_direction
    ) + 0.5 * lax.slice_in_dim(slopes, 0, extent - 3, axis=sweep_direction)
    state_right_side = lax.slice_in_dim(
        halo_extended_field, 2, extent - 1, axis=sweep_direction
    ) - 0.5 * lax.slice_in_dim(slopes, 1, extent - 2, axis=sweep_direction)
    advected_field_left = state_left_side[:, advected_field : advected_field + 1]
    advected_field_right = state_right_side[:, advected_field : advected_field + 1]
    signal_velocity = jnp.maximum(jnp.abs(advected_field_left), jnp.abs(advected_field_right))
    interface_fluxes = 0.5 * (
        advected_field_left * state_left_side + advected_field_right * state_right_side
    ) - 0.5 * signal_velocity * (state_right_side - state_left_side)
    return lax.slice_in_dim(
        interface_fluxes, 1, extent - 3, axis=sweep_direction
    ) - lax.slice_in_dim(interface_fluxes, 0, extent - 4, axis=sweep_direction)


def advance(halo_extended_field):
    centre = halo_extended_field[:, :, 2:-2]
    lat_div = flux_divergence(halo_extended_field, 2, 1)
    wrapped = jnp.concatenate([centre[..., -2:], centre, centre[..., :2]], axis=3)
    lon_div = flux_divergence(wrapped, 3, 0)
    return centre - COURANT * (lat_div + lon_div)


def obs_space(tile_state, obs_value, obs_site):
    site_count = tile_state.shape[2]
    ens_mean = jnp.mean(tile_state, axis=1)
    anomaly = tile_state - ens_mean[:, None, :]
    selector = (obs_site[:, :, None] == jnp.arange(site_count)[None, None, :]).astype(jnp.float32)
    obs_anomaly = jnp.einsum("bos,bks->bok", selector, anomaly, precision=HIGHEST)
    obs_mean = jnp.einsum("bos,bs->bo", selector, ens_mean, precision=HIGHEST)
    return (ens_mean, anomaly, obs_anomaly, obs_value - obs_mean)


def transform(local_anomaly, local_innovation, local_weight, ens_mean, anomaly):
    members = local_anomaly.shape[2]
    identity = jnp.eye(members, dtype=jnp.float32)
    weighted = local_anomaly * local_weight[:, :, None]
    gram_matrix = (
        jnp.einsum("bpk,bpj->bkj", weighted, local_anomaly, precision=HIGHEST)
        + (members - 1.0) * identity
    )
    frob_norm = jnp.sqrt(jnp.sum(gram_matrix * gram_matrix, axis=(1, 2)))
    root_iter = gram_matrix / frob_norm[:, None, None]
    inverse = jnp.broadcast_to(identity, gram_matrix.shape)
    for sweep in range(NSI):
        factor = 1.5 * identity - 0.5 * jnp.matmul(inverse, root_iter, precision=HIGHEST)
        root_iter = jnp.matmul(root_iter, factor, precision=HIGHEST)
        inverse = jnp.matmul(factor, inverse, precision=HIGHEST)
    projected = jnp.einsum("bpk,bp->bk", weighted, local_innovation, precision=HIGHEST)
    halfway = jnp.einsum("bkj,bj->bk", inverse, projected, precision=HIGHEST)
    mean_weights = (
        jnp.einsum("bkj,bj->bk", inverse, halfway, precision=HIGHEST) / frob_norm[:, None]
    )
    spread_weights = inverse * jnp.sqrt((members - 1.0) / frob_norm)[:, None, None]
    combined = spread_weights + mean_weights[:, :, None]
    return ens_mean[:, None, :] + jnp.einsum("bjk,bjs->bks", combined, anomaly, precision=HIGHEST)


def localise(obs_anomaly, innovation, slot_weight, neighbour_tiles, loc_weight, ens_mean, anomaly):
    batch_tiles = neighbour_tiles.shape[0]
    local_anomaly = obs_anomaly[neighbour_tiles].reshape(batch_tiles, -1, obs_anomaly.shape[2])
    local_innovation = innovation[neighbour_tiles].reshape(batch_tiles, -1)
    local_weight = (loc_weight[:, :, None] * slot_weight[neighbour_tiles]).reshape(batch_tiles, -1)
    return transform(local_anomaly, local_innovation, local_weight, ens_mean, anomaly)


def shards(ensemble, obs_value, obs_site, obs_count, obs_precision, loc_weight, neighbours):
    fields = ensemble
    lat_rows = fields.shape[2]
    margin = 2 * STEPS
    extended = extended_2(fields, (("band", 2),), margin)
    offset = lax.axis_index("band") * lat_rows
    lat_total = lat_rows * lax.axis_size("band")
    for repeat in range(STEPS):
        extended = advance(extended)
        remaining = margin - 2 * (repeat + 1)
        if remaining > 0:
            global_row = (
                lax.broadcasted_iota(jnp.int32, (1, 1, extended.shape[2], 1), 2)
                - remaining
                + offset
            )
            inside = (global_row >= 0) & (global_row < lat_total)
            extended = jnp.where(inside, extended, 0.0)
    fields = extended
    members, variables, lon_total = (fields.shape[0], fields.shape[1], fields.shape[3])
    flattened = fields.reshape(members, variables, lat_rows * lon_total)
    grouped = lax.all_to_all(flattened, "mem", split_axis=2, concat_axis=0, tiled=True)
    all_members = grouped.shape[0]
    tile_count = neighbours.shape[0]
    tile_state = (
        grouped.reshape(all_members, variables, tile_count, TILE)
        .transpose(2, 0, 1, 3)
        .reshape(tile_count, all_members, variables * TILE)
    )
    ens_mean, anomaly, obs_anomaly, innovation = obs_space(tile_state, obs_value, obs_site)
    live_slots = jnp.arange(obs_value.shape[1])[None, :] < obs_count[:, None]
    slot_weight = jnp.where(live_slots, obs_precision, 0.0)
    analysed = localise(
        obs_anomaly, innovation, slot_weight, neighbours, loc_weight, ens_mean, anomaly
    )
    outgoing = (
        analysed.reshape(tile_count, all_members, variables, TILE)
        .transpose(1, 2, 0, 3)
        .reshape(all_members, variables, tile_count * TILE)
    )
    returned = lax.all_to_all(outgoing, "mem", split_axis=0, concat_axis=2, tiled=True)
    fields = returned.reshape(members, variables, lat_rows, lon_total)
    return advance(extended_2(fields, (("band", 2),), 2))


def split_pair(x):
    high = x.astype(jnp.bfloat16)
    low = (x - high.astype(jnp.float32)).astype(jnp.bfloat16)
    return high, low


def left_form(x):
    return jnp.concatenate(split_pair(x), axis=1)


def right_form(x):
    wide = jnp.concatenate(split_pair(x), axis=1)
    return jnp.concatenate([wide, wide], axis=0)


def pair_dot(left, right):
    both = jnp.dot(left, right, preferred_element_type=jnp.float32)
    half = both.shape[1] // 2
    return both[:, :half] + both[:, half:]


def upwind(left, right, carrier):
    a_left = left[carrier : carrier + 1]
    a_right = right[carrier : carrier + 1]
    speed = jnp.maximum(jnp.abs(a_left), jnp.abs(a_right))
    return 0.5 * (a_left * left + a_right * right) - 0.5 * speed * (right - left)


def lon_divergence(row):
    size = row.shape[2]
    jump = pltpu.roll(row, size - 1, 2) - row
    half = 0.5 * minmod(pltpu.roll(jump, 1, 2), jump)
    flux = upwind(row + half, pltpu.roll(row - half, size - 1, 2), 0)
    return flux - pltpu.roll(flux, 1, 2)


def advance_rows(load, store, count):
    rows = [load(i) for i in range(4)]
    jumps = [rows[i + 1] - rows[i] for i in range(3)]
    halves = [0.5 * minmod(jumps[i], jumps[i + 1]) for i in range(2)]
    lower = upwind(rows[1] + halves[0], rows[2] - halves[1], 1)
    for k in range(count):
        ahead = load(k + 4)
        jump = ahead - rows[3]
        half = 0.5 * minmod(jumps[2], jump)
        upper = upwind(rows[2] + halves[1], rows[3] - half, 1)
        centre = rows[2]
        change = (upper - lower) + lon_divergence(centre)
        store(k, centre - COURANT * change)
        rows = rows[1:] + [ahead]
        jumps = jumps[1:] + [jump]
        halves = [halves[1], half]
        lower = upper


def cycle_kernel(
    bands,
    mems,
    loc_ref,
    near_ref,
    count_ref,
    x_ref,
    value_ref,
    site_ref,
    precision_ref,
    out_ref,
    first,
    second,
    third,
    state,
    weight_buf,
    target_buf,
    anomaly,
    means,
    gram,
    pull,
    root,
    inverse,
    turned,
    result,
    final,
    send_a,
    recv_a,
    send_b,
    recv_b,
    send_d,
    recv_d,
    local_sem,
):
    band = lax.axis_index("band")
    mem = lax.axis_index("mem")
    side = lax.rem(band, 2)
    base = band - side
    lon = x_ref.shape[1]
    half = state.shape[2]
    group = 2 * half
    nv = state.shape[1]
    lat = x_ref.shape[0] // (group * nv)
    span = nv * lat
    tiles = lon // TILE
    members = group * mems
    sites = nv * TILE
    me = side * mems + mem

    def greet(b, m, okay):
        @pl.when(okay)
        def _():
            pl.semaphore_signal(
                barrier, inc=1, device_id={"band": b, "mem": m}, device_id_type=MESH
            )

        return okay.astype(jnp.int32) if hasattr(okay, "astype") else jnp.int32(okay)

    barrier = pltpu.get_barrier_semaphore()
    partners = jnp.int32(0)
    for k in range(2 * mems):
        partners += greet(base + k // mems, jnp.int32(k % mems), me != k)
    near_band = jnp.where(side == 0, base - 1, base + 2)
    near_okay = (near_band >= 0) & (near_band < bands)
    for m in range(mems):
        partners += greet(near_band, jnp.int32(m), near_okay)
    past_band = jnp.where(side == 0, base - 2, base + 3)
    partners += greet(past_band, mem, near_okay)
    other_band = jnp.where(side == 0, base + 2, base - 1)
    other_okay = (other_band >= 0) & (other_band < bands)
    partners += greet(other_band, mem, other_okay)
    slots = value_ref.shape[1]
    slot_index = lax.broadcasted_iota(jnp.int32, (1, slots), 1)
    site_index = lax.broadcasted_iota(jnp.int32, (sites, slots), 0)
    for u in range(tiles):
        match = site_index == site_ref[u : u + 1, :]
        live = slot_index < count_ref[0, u]
        precision = jnp.where(live, precision_ref[u : u + 1, :], 0.0)
        weighted_value = precision * value_ref[u : u + 1, :]
        total = jnp.sum(jnp.where(match, precision, 0.0), axis=1, keepdims=True)
        weight_buf[u] = jnp.broadcast_to(total, (sites, members))
        total = jnp.sum(jnp.where(match, weighted_value, 0.0), axis=1, keepdims=True)
        target_buf[u] = jnp.broadcast_to(total, (sites, members))

    pl.semaphore_wait(barrier, partners)

    chunks = 4
    depth = half * span // chunks

    def copy_a(src, place, c, sem, target):
        return pltpu.make_async_remote_copy(
            src_ref=src,
            dst_ref=first.at[place, pl.ds(c * depth, depth), :],
            send_sem=send_a.at[sem, c],
            recv_sem=recv_a.at[place, c],
            device_id={"band": target, "mem": mem},
            device_id_type=MESH,
        )

    def own_part(h, c):
        return x_ref.at[pl.ds(h * half * span + c * depth, depth), :]

    own_a = pltpu.make_async_copy(
        x_ref.at[pl.ds(side * half * span, half * span), :], first.at[1 + side], local_sem.at[0]
    )
    partner = base + 1 - side
    got = 2 - side
    to_pair = [copy_a(own_part(1 - side, c), 1 + side, c, 0, partner) for c in range(chunks)]
    to_past = [copy_a(own_part(side, c), 3 - 3 * side, c, 1, past_band) for c in range(chunks)]
    relayed = [
        copy_a(first.at[got, pl.ds(c * depth, depth), :], 3 * side, c, 2, other_band)
        for c in range(chunks)
    ]

    for copy in to_pair:
        copy.start()

    @pl.when(near_okay)
    def _():
        for copy in to_past:
            copy.start()

    own_a.start()

    zeros = jnp.zeros((half * span, lon), jnp.float32)

    @pl.when(base == 0)
    def _():
        first[0] = zeros

    @pl.when(base == bands - 2)
    def _():
        first[3] = zeros

    def arrive(place, c):
        copy_a(own_part(side, c), place, c, 0, partner).wait_recv()

    for c in range(chunks):
        arrive(got, c)

        @pl.when(other_okay)
        def _():
            relayed[c].start()

    own_a.wait()
    edge = 2
    low_mask = jnp.where(base > 0, 1.0, 0.0)
    high_mask = jnp.where(base < bands - 2, 1.0, 0.0)
    block = 8
    parts = half // block

    def copy_b(part, k, sender):
        some = pl.ds(part * block, block)
        return pltpu.make_async_remote_copy(
            src_ref=third.at[k, :, some, :],
            dst_ref=state.at[sender, :, some, :],
            send_sem=send_b.at[part, k],
            recv_sem=recv_b.at[part, sender],
            device_id={"band": base + k // mems, "mem": jnp.int32(k % mems)},
            device_id_type=MESH,
        )

    def forecast_part(part):
        some = pl.ds(part * block, block)
        ready = range(part * chunks // parts, (part + 1) * chunks // parts)

        @pl.when(base > 0)
        def _():
            for c in ready:
                arrive(0, c)

        @pl.when(base < bands - 2)
        def _():
            for c in ready:
                arrive(3, c)

        def load_first(i):
            start = part * block * span + i % lat
            return jnp.stack(
                [first[i // lat, pl.ds(start + v * lat, block, stride=span), :] for v in range(nv)]
            )

        def store_second(k, row):
            if k < lat - edge:
                row = row * low_mask
            if k >= 3 * lat - edge:
                row = row * high_mask
            second[k, :, some, :] = row

        def store_third(k, row):
            third[k, :, some, :] = row

            @pl.when(me != k)
            def _():
                copy_b(part, k, me).start()

            @pl.when(me == k)
            def _():
                state[me, :, some, :] = row

        advance_rows(load_first, store_second, 4 * lat - 2 * edge)
        advance_rows(lambda i: second[i, :, some, :], store_third, 2 * lat)

    for part in range(parts):
        forecast_part(part)

    for part in range(parts):
        for k in range(2 * mems):

            @pl.when(me != k)
            def _():
                copy_b(part, k, jnp.int32(k)).wait_recv()

    for v in range(nv):
        pieces = [state[(k % 2) * mems + k // 2, v] for k in range(2 * mems)]
        field = jnp.concatenate(pieces, axis=0).T
        mean = jnp.mean(field, axis=1, keepdims=True)
        means[v] = jnp.broadcast_to(mean, (lon, members))
        anomaly[v] = field - mean

    def of_tile(ref, u):
        return jnp.concatenate([ref[v, u * TILE : (u + 1) * TILE, :] for v in range(nv)], axis=0)

    for u in range(tiles):
        p = of_tile(anomaly, u)
        d = weight_buf[u]
        p_high, p_low = split_pair(p)
        w_high, w_low = split_pair(p * d)
        gram[u] = lax.dot_general(
            jnp.concatenate([w_high, w_low, w_high], axis=0),
            jnp.concatenate([p_high, p_high, p_low], axis=0),
            (((0,), (0,)), ((), ())),
            preferred_element_type=jnp.float32,
        )
        pull[u] = jnp.sum(p * (target_buf[u] - d * of_tile(means, u)), axis=0, keepdims=True)

    identity = (
        lax.broadcasted_iota(jnp.int32, (members, members), 0)
        == lax.broadcasted_iota(jnp.int32, (members, members), 1)
    ).astype(jnp.float32)
    listed = near_ref.shape[0]
    norms = []
    drives = []
    for t in range(tiles):
        a = (members - 1.0) * identity
        drive = jnp.zeros((1, members), jnp.float32)
        for j in range(listed):
            u = near_ref[j, t]
            scale = loc_ref[j, t]
            a += scale * gram[u]
            drive += scale * pull[u]
        norm = jnp.sqrt(jnp.sum(jnp.sum(a * a, axis=1, keepdims=True), axis=0, keepdims=True))
        norms.append(norm)
        drives.append(drive)
        r = a * (1.0 / norm)
        s = 1.5 * identity - 0.5 * r
        root[t] = pair_dot(left_form(r), right_form(s))
        inverse[t] = s

    width = lon // CUTS
    packed = group // CUTS

    def copy_d(cut, m, place, sem, target):
        return pltpu.make_async_remote_copy(
            src_ref=result.at[cut, :, pl.ds(m * group, packed), :],
            dst_ref=final.at[place, cut],
            send_sem=send_d.at[cut, sem],
            recv_sem=recv_d.at[cut, place],
            device_id={"band": target, "mem": jnp.int32(m)},
            device_id_type=MESH,
        )

    outward = 1 - 2 * (mem < edge).astype(jnp.int32)
    out_band = band + outward
    out_okay = (out_band >= 0) & (out_band < bands)
    out_place = mem + edge - outward * lat

    def own_d(cut):
        return pltpu.make_async_copy(
            result.at[cut, :, pl.ds(mem * group, packed), :],
            final.at[mem + edge, cut],
            local_sem.at[1 + cut],
        )

    blank = jnp.zeros((edge, CUTS, nv, packed, lon), jnp.float32)

    @pl.when(band == 0)
    def _():
        final[0:edge] = blank

    @pl.when(band == bands - 1)
    def _():
        final[lat + edge : lat + 2 * edge] = blank

    def analyse_cut(cut):
        chosen = range(cut * tiles // CUTS, (cut + 1) * tiles // CUTS)

        def sweep(_, carry):
            for t in chosen:
                r, z = root[t], inverse[t]
                r_left, r_right = left_form(r), right_form(r)
                s = 1.5 * identity - 0.5 * pair_dot(left_form(z), r_right)
                root[t] = pair_dot(r_left, right_form(s))
                inverse[t] = pair_dot(left_form(s), right_form(z))
            return carry

        lax.fori_loop(0, NSI - 2, sweep, 0, unroll=True)

        for t in chosen:
            r, z = root[t], inverse[t]
            s = 1.5 * identity - 0.5 * pair_dot(left_form(z), right_form(r))
            z = pair_dot(left_form(s), right_form(z))
            p = of_tile(anomaly, t)
            stacked = jnp.concatenate([p, jnp.broadcast_to(drives[t], (TILE, members))], axis=0)
            applied = pair_dot(left_form(stacked), right_form(z))
            q = applied[:sites]
            step = applied[sites : sites + 1]
            shift = jnp.sum(q * step, axis=1, keepdims=True) / norms[t]
            new = of_tile(means, t) + q * jnp.sqrt((members - 1.0) / norms[t]) + shift
            for v in range(nv):
                turned[v, t * TILE : (t + 1) * TILE, :] = new[v * TILE : (v + 1) * TILE, :]

        for v in range(nv):
            cells = turned[v, cut * width : (cut + 1) * width, :]
            shifted = [cells] + [
                pltpu.roll(cells, members - k * packed, 1) for k in range(1, CUTS)
            ]
            result[cut, v] = jnp.concatenate(shifted, axis=0).T

        for m in range(mems):

            @pl.when(out_okay)
            def _():
                copy_d(cut, m, out_place, mems + m, out_band).start()

        for m in range(mems):

            @pl.when(mem != m)
            def _():
                copy_d(cut, m, mem + edge, m, band).start()

        own_d(cut).start()

    for cut in range(CUTS):
        analyse_cut(cut)

    for cut in range(CUTS):
        own_d(cut).wait()
        for k in range(lat + 2 * edge):
            if k < edge:
                okay = band > 0
            elif k < lat + edge:
                okay = mem != k - edge
            else:
                okay = band < bands - 1

            @pl.when(okay)
            def _():
                copy_d(cut, 0, k, 0, band).wait_recv()

    strip = lax.broadcasted_iota(jnp.int32, (1, 1, lon), 2) // width

    def load_final(i):
        cuts = [final[i, cut] for cut in range(CUTS)]
        pieces = []
        for k in range(CUTS):
            piece = None
            for cut in range(CUTS):
                placed = cuts[cut]
                if cut != k:
                    placed = pltpu.roll(placed, ((cut - k) * width) % lon, 2)
                piece = placed if piece is None else jnp.where(strip == cut, placed, piece)
            pieces.append(piece)
        return jnp.concatenate(pieces, axis=1)

    def store_out(k, row):
        for v in range(nv):
            out_ref[pl.ds(v * lat + k, group, stride=span), :] = row[v]

    advance_rows(load_final, store_out, lat)

    for copy in to_pair:
        copy.wait_send()

    @pl.when(near_okay)
    def _():
        for copy in to_past:
            copy.wait_send()

    @pl.when(other_okay)
    def _():
        for copy in relayed:
            copy.wait_send()

    for part in range(parts):
        for k in range(2 * mems):

            @pl.when(me != k)
            def _():
                copy_b(part, k, me).wait_send()

    for cut in range(CUTS):
        for m in range(mems):

            @pl.when(out_okay)
            def _():
                copy_d(cut, m, out_place, mems + m, out_band).wait_send()

            @pl.when(mem != m)
            def _():
                copy_d(cut, m, mem + edge, m, band).wait_send()


def fused_shards(
    bands, mems, ensemble, obs_value, obs_site, obs_count, obs_precision, loc_weight, neighbours
):
    group, nv, lat, lon = ensemble.shape
    half = group // 2
    tiles = lon // TILE
    members = group * mems
    sites = nv * TILE
    edge = 2
    f32 = jnp.float32
    vmem = pl.BlockSpec(memory_space=pltpu.VMEM)
    smem = pl.BlockSpec(memory_space=pltpu.SMEM)
    rows = pl.pallas_call(
        functools.partial(cycle_kernel, bands, mems),
        out_shape=jax.ShapeDtypeStruct((group * nv * lat, lon), f32),
        in_specs=[smem] * 3 + [pl.BlockSpec(memory_space=pl.ANY)] + [vmem] * 3,
        out_specs=vmem,
        scratch_shapes=[
            pltpu.VMEM((4, half * nv * lat, lon), f32),
            pltpu.VMEM((4 * lat - 2 * edge, nv, half, lon), f32),
            pltpu.VMEM((2 * lat, nv, half, lon), f32),
            pltpu.VMEM((2 * mems, nv, half, lon), f32),
            pltpu.VMEM((tiles, sites, members), f32),
            pltpu.VMEM((tiles, sites, members), f32),
            pltpu.VMEM((nv, lon, members), f32),
            pltpu.VMEM((nv, lon, members), f32),
            pltpu.VMEM((tiles, members, members), f32),
            pltpu.VMEM((tiles, 1, members), f32),
            pltpu.VMEM((tiles, members, members), f32),
            pltpu.VMEM((tiles, members, members), f32),
            pltpu.VMEM((nv, lon, members), f32),
            pltpu.VMEM((CUTS, nv, members, lon), f32),
            pltpu.VMEM((lat + 2 * edge, CUTS, nv, group // CUTS, lon), f32),
            pltpu.SemaphoreType.DMA((3, 4)),
            pltpu.SemaphoreType.DMA((4, 4)),
            pltpu.SemaphoreType.DMA((half // 8, 2 * mems)),
            pltpu.SemaphoreType.DMA((half // 8, 2 * mems)),
            pltpu.SemaphoreType.DMA((CUTS, 2 * mems)),
            pltpu.SemaphoreType.DMA((CUTS, lat + 2 * edge)),
            pltpu.SemaphoreType.DMA((1 + CUTS,)),
        ],
        compiler_params=pltpu.CompilerParams(collective_id=0, has_side_effects=True),
    )(
        loc_weight.T,
        neighbours.T,
        obs_count[None, :],
        ensemble.reshape(group * nv * lat, lon),
        obs_value,
        obs_site,
        obs_precision,
    )
    return rows.reshape(ensemble.shape)


def solution(mesh):
    bands, mems = mesh.shape["band"], mesh.shape["mem"]

    def body(ensemble, *rest):
        group, _, lat, lon = ensemble.shape
        fits = (
            STEPS == 2
            and lat == 4
            and lat == mems
            and bands % 2 == 0
            and group % 16 == 0
            and lon == group * mems == 128
        )
        if fits:
            return fused_shards(bands, mems, ensemble, *rest)
        return shards(ensemble, *rest)

    return jax.shard_map(
        body,
        mesh=mesh,
        in_specs=(
            P("mem", None, "band", None),
            P(("band", "mem"), None),
            P(("band", "mem"), None),
            P(("band", "mem")),
            P(("band", "mem"), None),
            P(("band", "mem"), None),
            P(("band", "mem"), None),
        ),
        out_specs=P("mem", None, "band", None),
        check_vma=False,
    )
```
